128 devices in a mesh: lev: 8 (over x, z_lo), mem: 16 (over z_hi, y, core).
Axes of the slice: x: 4, y: 4, z: 4 (z_hi: 2, z_lo: 2; z = z_hi * 2 + z_lo), core: 2. Of those that a mesh axis runs over, the one named last changes fastest.
Arguments:
- control: float32 [4096, 128, 128], P(None, 'mem', 'lev'), may hold values from -6 to 6
- perturb: bfloat16 [4096, 128, 5, 128], P('lev', 'mem'), may hold values from -6 to 6
- member_weights: float32 [128], P('mem'), may hold values from 0.25 to 4
- blocks: bfloat16 [64, 16, 64, 64], P(None, 'mem'), may hold values from -0.1875 to 0.1875
- block_cols: int32 [64, 16], replicated, may hold values from 0 to 63, as said below
- vertical: float32 [128, 128], replicated, may hold values from -4 to 4
Outputs:
- increment: float32 [4096, 5, 128], P(('lev', 'mem'))
The draws below stay inside these ranges and needn't reach their ends.
Inputs may be any that keep to these rules, and one draw needn't show every extreme that they name: Within a block row the 16 block columns are distinct, and for every j the column block_cols[:, j] names each of the 64 block rows exactly once.
All inputs are finite; a program needn't handle non-finite values.
Results may differ from the reference program's by a relative error of at most 0.0003.
Values may be sent and summed in bfloat16 or wider, within the bound.
No kernel may reach another device: no remote copies, remote signals or barrier semaphores. Data moves between devices by JAX's collectives and lax.ppermute only.
A program may use at most 192 MiB of HBM per device.

```python
import math
import jax
import jax.numpy as jnp
from jax import lax

NB = 64
BS = 64
LEV = 128
NVAR = 5
KB = 16
NODES = 4096
MEMBERS = 128


def draw_block_cols(key, part):
    base_key = jax.random.fold_in(key, 11)
    key_outer, key_inner, key_offset = jax.random.split(base_key, 3)
    outer_perm = jax.random.permutation(key_outer, NB)
    inner_perm = jax.random.permutation(key_inner, NB)
    offsets = jax.random.permutation(key_offset, 2 * KB)[:KB] - KB
    shifted = (inner_perm[:, None] + offsets[None, :]) % NB
    return outer_perm[shifted].astype(jnp.int32)


def draw_vertical(key, part):
    base_key = jax.random.fold_in(key, 23)
    key_rough = jax.random.fold_in(base_key, 0)
    levels_iota = jnp.arange(LEV)
    distance = jnp.abs(levels_iota[:, None] - levels_iota[None, :]).astype(jnp.float32)
    reach = jnp.float32(LEV / 8.0)
    envelope = jnp.exp(-distance / reach)
    rough = 0.4 * jnp.clip(jax.random.normal(key_rough, (LEV, LEV), jnp.float32), -4.0, 4.0)
    matrix = jnp.eye(LEV, dtype=jnp.float32) + rough * envelope
    return matrix.astype(jnp.float32)


def strengthened(entries, rng, source, target, shards_of, factor):
    def block_of(dim):
        return (jnp.arange(entries.shape[dim]) // (entries.shape[dim] // shards_of)).reshape((-1,) + (1,) * (entries.ndim - 1 - dim))

    one_side = jax.random.permutation(rng, shards_of)[block_of(target)]
    far = (block_of(target) + shards_of // 2) % shards_of
    return jnp.where((block_of(source) == one_side) | (block_of(source) == far), factor * entries, entries)


def levels(stream_key, dims, pieces, smallest, top_value):
    def one(position, parts):
        steps = jax.random.uniform(jax.random.fold_in(jax.random.fold_in(stream_key, 6), position), (parts,), jnp.float32, smallest / len(pieces), top_value / len(pieces))
        return jnp.repeat(jnp.exp(steps), dims[position] // parts).reshape((-1,) + (1,) * (len(dims) - position - 1))

    gain = one(*pieces[0])
    for cut in pieces[1:]:
        gain = gain * one(*cut)
    return gain


def gaussian(key, dims, scale, limit, pieces=(), held_as=jnp.bfloat16):
    entries = scale * jax.random.normal(key, dims, jnp.float32)
    if pieces:
        entries = entries * levels(key, dims, pieces, -0.22, 0.18)
    return jnp.clip(entries, -limit, limit).astype(held_as)


def noise_with(own_key, shape, spread, limit, shards, heavy, kind=jnp.bfloat16):
    result = spread * jax.random.normal(own_key, shape, jnp.float32)
    if shards:
        result = result * levels(own_key, shape, shards, -0.22, 0.18)
    return jnp.clip(strengthened(result, jax.random.fold_in(own_key, 3), *heavy), -limit, limit).astype(kind)


def setup_inputs(seed: int = 0) -> dict:
    key_list = jax.random.split(jax.random.key(seed), 7)
    control = gaussian(key_list[0], (NODES, MEMBERS, LEV), 1.0, 6.0, ((1, 16), (2, 8)), jnp.float32)
    perturb = noise_with(key_list[1], (NODES, MEMBERS, NVAR, LEV), 1.0, 6.0, ((0, 8), (1, 16)), (1, 0, 16, 2.0))
    member_weights = jnp.clip(jnp.exp(math.log(4.0) - 2.7725887 * jax.random.uniform(key_list[2], (MEMBERS,), jnp.float32) ** levels(key_list[2], (MEMBERS,), ((0, 16),), -0.2, 0.2)), 0.25, 4.0)
    blocks = gaussian(key_list[3], (NB, KB, BS, BS), (KB * BS) ** -0.5, 0.1875, ((1, 16),))
    block_cols = draw_block_cols(jax.random.fold_in(key_list[6], 71), 0)
    vertical = draw_vertical(jax.random.fold_in(key_list[6], 71), 0)
    return {"control": control, "perturb": perturb, "member_weights": member_weights, "blocks": blocks, "block_cols": block_cols, "vertical": vertical}


def reference(control, perturb, member_weights, blocks, block_cols, vertical):
    block_tiles = blocks.astype(jnp.float32)
    scaled_weights = member_weights / math.sqrt(MEMBERS - 1)

    def member_step(summed, member):
        member_field = lax.dynamic_index_in_dim(control, member, 1, keepdims=False).reshape(NB, BS, LEV)
        forward_sum = jnp.zeros((NB, BS, LEV), jnp.float32)
        for stored in range(KB):
            chosen = member_field[block_cols[:, stored]]
            forward_sum = forward_sum + jnp.einsum('ipq,iql->ipl', block_tiles[:, stored], chosen, precision=lax.Precision.HIGHEST)
        backward_sum = jnp.zeros((NB, BS, LEV), jnp.float32)
        for stored in range(KB):
            product = jnp.einsum('ipq,ipl->iql', block_tiles[:, stored], forward_sum, precision=lax.Precision.HIGHEST)
            backward_sum = backward_sum.at[block_cols[:, stored]].add(product)
        localized = jnp.dot(backward_sum.reshape(NODES, LEV), vertical.T, precision=lax.Precision.HIGHEST, preferred_element_type=jnp.float32)
        localized = localized * scaled_weights[member]
        perturbation = lax.dynamic_index_in_dim(perturb, member, 1, keepdims=False).astype(jnp.float32)
        return (summed + perturbation * localized[:, None, :], None)
    start_sum = jnp.zeros((NODES, NVAR, LEV), jnp.float32)
    increment, unused = lax.scan(member_step, start_sum, jnp.arange(MEMBERS, dtype=jnp.int32))
    return increment
```

```python
import functools
import math

import jax
import jax.numpy as jnp
from jax import lax
from jax.experimental import pallas as pl
from jax.experimental.pallas import tpu as pltpu
from jax.sharding import PartitionSpec as P

BF = jnp.bfloat16
F32 = jnp.float32
AXES = ("lev", "mem")


def coords(d):
    lev, mem = divmod(d, 16)
    x, zlo = divmod(lev, 2)
    zhi, rest = divmod(mem, 8)
    y, c = divmod(rest, 2)
    return x, y, 2 * zhi + zlo, c


def device(x, y, z, c):
    zhi, zlo = divmod(z % 4, 2)
    return ((x % 4) * 2 + zlo) * 16 + zhi * 8 + (y % 4) * 2 + c


def perm(move):
    return [(d, device(*move(*coords(d)))) for d in range(128)]


Z_NEAR = perm(lambda x, y, z, c: (x, y, 3 - z, c))
Y_UP = perm(lambda x, y, z, c: (x, y + 1, z, c))
Y_DOWN = perm(lambda x, y, z, c: (x, y - 1, z, c))
CORE = perm(lambda x, y, z, c: (x, y, z, 1 - c))


def send(value, pairs):
    return lax.ppermute(value, AXES, pairs)


def split2(x):
    hi = x.astype(BF)
    return hi, (x - hi.astype(F32)).astype(BF)


def pack_kernel(b_ref, o_ref):
    for t in range(b_ref.shape[0] // 2):
        two = jnp.concatenate([b_ref[2 * t], b_ref[2 * t + 1]], axis=0).astype(F32)
        o_ref[t] = two.T.astype(BF)


def pack(b):
    n, p, q = b.shape
    return pl.pallas_call(pack_kernel, out_shape=jax.ShapeDtypeStruct((n // 2, q, 2 * p), BF))(b)


def main_kernel(starts, cols_ref, jtab_ref, x_ref, *rest):
    pieces = rest[: len(starts)]
    y_ref, bt, xc, fc = rest[len(starts) :]
    n_all = bt.shape[0]
    half_cols = x_ref.shape[0]
    width = y_ref.shape[2]

    def zero(r, _):
        bt[pl.ds(pl.multiple_of(r * 64, 64), 64), :] = jnp.zeros((64, n_all), BF)
        return 0

    lax.fori_loop(0, n_all // 64, zero, 0)

    def split(c, _):
        s = pl.ds(pl.multiple_of(c * 512, 512), 512)
        hi, lo = split2(x_ref[:, s])
        xc[0:half_cols, s] = hi
        xc[half_cols:, s] = lo
        return 0

    lax.fori_loop(0, n_all // 512, split, 0)
    for slot, (piece, start) in enumerate(zip(pieces, starts)):
        j = jtab_ref[slot]
        for t in range(piece.shape[0]):
            both = piece[t]
            for h in range(2):
                i = 2 * (start + t) + h
                row = pl.ds(pl.multiple_of(cols_ref[i, j] * 64, 64), 64)
                bt[row, i * 64 : (i + 1) * 64] = both[:, h * 64 : h * 64 + 64]

    def forward(n, _):
        s = pl.ds(pl.multiple_of(n * 256, 256), 256)
        f = jnp.dot(xc[...], bt[:, s], preferred_element_type=F32)
        hi, lo = split2(f[:half_cols] + f[half_cols:])
        fc[0:half_cols, s] = hi
        fc[half_cols:, s] = lo
        return 0

    lax.fori_loop(0, n_all // 256, forward, 0)

    def backward(n, _):
        s = pl.ds(pl.multiple_of(n * 256, 256), 256)
        y = lax.dot_general(
            fc[...], bt[s, :], (((1,), (1,)), ((), ())), preferred_element_type=F32
        )
        per = width // 256
        inside = pl.ds(pl.multiple_of(lax.rem(n, per) * 256, 256), 256)
        y_ref[n // per, :, inside] = y[:half_cols] + y[half_cols:]
        return 0

    lax.fori_loop(0, n_all // 256, backward, 0)


def main_call(cols, jtab, x, pieces, starts):
    columns, n_all = x.shape
    vm = pl.BlockSpec(memory_space=pltpu.VMEM)
    sm = pl.BlockSpec(memory_space=pltpu.SMEM)
    return pl.pallas_call(
        functools.partial(main_kernel, starts),
        out_shape=jax.ShapeDtypeStruct((8, columns, n_all // 8), F32),
        in_specs=[sm, sm, vm] + [vm] * len(pieces),
        out_specs=vm,
        scratch_shapes=[
            pltpu.VMEM((n_all, n_all), BF),
            pltpu.VMEM((2 * columns, n_all), BF),
            pltpu.VMEM((2 * columns, n_all), BF),
        ],
        compiler_params=pltpu.CompilerParams(vmem_limit_bytes=60 * 1024 * 1024),
    )(cols, jtab, x, *pieces)


def post_kernel(w_ref, y_ref, v_ref, p_ref, o_ref, loc):
    groups, members, _, _ = y_ref.shape
    vhi, vlo = split2(v_ref[...])
    dims = (((1,), (1,)), ((), ()))
    for k in range(members):
        column = jnp.concatenate([y_ref[s, k] for s in range(groups)], axis=0)
        hi, lo = split2(column.T)
        part = lax.dot_general(hi, vhi, dims, preferred_element_type=F32)
        part += lax.dot_general(lo, vhi, dims, preferred_element_type=F32)
        part += lax.dot_general(hi, vlo, dims, preferred_element_type=F32)
        loc[:, k, :] = part * w_ref[k]
    for d in range(o_ref.shape[0]):
        rows = pl.ds(d * o_ref.shape[2], o_ref.shape[2])
        for v in range(o_ref.shape[1]):
            o_ref[d, v] = jnp.sum(p_ref[rows, v].astype(F32) * loc[rows], axis=1)


def post_call(w, y, v, p, block, owned):
    n, nvar, members, levels = p.shape
    groups, _, inner, _ = y.shape
    return pl.pallas_call(
        post_kernel,
        grid=(n // block,),
        out_shape=jax.ShapeDtypeStruct((n // owned, nvar, owned, levels), F32),
        in_specs=[
            pl.BlockSpec(memory_space=pltpu.SMEM),
            pl.BlockSpec((groups, members, inner, block), lambda g: (0, 0, 0, g)),
            pl.BlockSpec((levels, levels), lambda g: (0, 0)),
            pl.BlockSpec((block, nvar, members, levels), lambda g: (g, 0, 0, 0)),
        ],
        out_specs=pl.BlockSpec((block // owned, nvar, owned, levels), lambda g: (g, 0, 0, 0)),
        scratch_shapes=[pltpu.VMEM((block, members, levels), F32)],
    )(w, y, v, p)


def gather(own):
    half = own.shape[0] // 2
    near = send(own, Z_NEAR)
    up = send(own, Y_UP)
    down = send(own, Y_DOWN)
    far_a = send(up[:half], Y_UP)
    far_b = send(down[half:], Y_DOWN)
    near_up = send(near, Y_UP)
    near_down = send(near, Y_DOWN)
    near_far_a = send(near_up[:half], Y_UP)
    near_far_b = send(near_down[half:], Y_DOWN)
    parts = [
        (own, 0, 0, 0),
        (near, 0, 0, 1),
        (up, 0, 3, 0),
        (down, 0, 1, 0),
        (far_a, 0, 2, 0),
        (far_b, half, 2, 0),
        (near_up, 0, 3, 1),
        (near_down, 0, 1, 1),
        (near_far_a, 0, 2, 1),
        (near_far_b, half, 2, 1),
    ]
    pieces, starts, slots = [], [], []
    mem = lax.axis_index("mem")
    zhi, y, c = mem // 8, (mem // 2) % 4, mem % 2
    for value, start, dy, dz in parts:
        j = ((zhi + dz) % 2) * 8 + ((y + dy) % 4) * 2
        for swap in (0, 1):
            pieces.append(send(value, CORE) if swap else value)
            starts.append(start)
            slots.append(j + (c + swap) % 2)
    return pieces, tuple(starts), jnp.stack(slots).astype(jnp.int32)


def shards(control, perturb, member_weights, blocks, block_cols, vertical):
    nodes_all, mem_dev, lev_dev = control.shape
    mem_size = lax.axis_size("mem")
    own = pack(blocks[:, 0])
    pieces, starts, jtab = gather(own)
    x = control.transpose(1, 2, 0).reshape(mem_dev * lev_dev, nodes_all)
    y = main_call(block_cols, jtab, x, pieces, starts)
    y = y.reshape(8, mem_dev, lev_dev, nodes_all // 8)
    y = lax.all_to_all(y, "lev", split_axis=0, concat_axis=0, tiled=True)
    weights = member_weights / math.sqrt(mem_dev * mem_size - 1)
    owned = nodes_all // 128
    out = post_call(weights, y, vertical, perturb.transpose(0, 2, 1, 3), 128, owned)
    out = lax.all_to_all(out, "mem", split_axis=0, concat_axis=0, tiled=True)
    return jnp.sum(out, axis=0).transpose(1, 0, 2)


def solution(mesh):
    in_specs = (
        P(None, "mem", "lev"),
        P("lev", "mem", None, None),
        P("mem"),
        P(None, "mem", None, None),
        P(),
        P(),
    )
    out_specs = P(("lev", "mem"), None, None)
    return jax.shard_map(shards, mesh=mesh, in_specs=in_specs, out_specs=out_specs, check_vma=False)
```

```python
import functools
import math

import jax
import jax.numpy as jnp
from jax import lax
from jax.experimental import pallas as pl
from jax.experimental.pallas import tpu as pltpu
from jax.sharding import Mesh
from jax.sharding import PartitionSpec as P

BF = jnp.bfloat16
F32 = jnp.float32
AXES = ("x", "zlo", "zhi", "y", "core")
CHUNKS = 1


def coords(d):
    x, zlo, zhi, y, c = d // 32, d // 16 % 2, d // 8 % 2, d // 2 % 4, d % 2
    return x, y, 2 * zhi + zlo, c


def device(x, y, z, c):
    return (x % 4) * 32 + (z % 2) * 16 + (z // 2) * 8 + (y % 4) * 2 + c


def perm(move):
    return [(d, device(*move(*coords(d)))) for d in range(128)]


Z_NEAR = perm(lambda x, y, z, c: (x, y, 3 - z, c))
Y_UP = perm(lambda x, y, z, c: (x, y + 1, z, c))
Y_DOWN = perm(lambda x, y, z, c: (x, y - 1, z, c))
CORE = perm(lambda x, y, z, c: (x, y, z, 1 - c))
VMEM = pl.BlockSpec(memory_space=pltpu.VMEM)
SMEM = pl.BlockSpec(memory_space=pltpu.SMEM)


def send(value, pairs):
    return lax.ppermute(value, AXES, pairs)


def split2(x):
    hi = x.astype(BF)
    return hi, (x - hi.astype(F32)).astype(BF)


def pack_kernel(core_ref, b_ref, keep_ref, give_ref):
    rows = keep_ref.shape[0]
    for out, half in ((give_ref, 1 - core_ref[0]), (keep_ref, core_ref[0])):
        for t in range(rows):
            i = 2 * (half * rows + t)
            two = jnp.concatenate([b_ref[i], b_ref[i + 1]], axis=0).astype(F32)
            out[t] = two.T.astype(BF)


def pack(core, b):
    n, p, q = b.shape
    shape = jax.ShapeDtypeStruct((n // 4, q, 2 * p), BF)
    return pl.pallas_call(
        pack_kernel, out_shape=(shape, shape), in_specs=[SMEM, VMEM], out_specs=(VMEM, VMEM)
    )(core, b)


def prep_kernel(core_ref, own_ref, other_ref, o_ref):
    core = core_ref[0]
    columns, width = own_ref.shape
    for ref, c in ((own_ref, core), (other_ref, 1 - core)):
        value = ref[...]
        for owner in range(2):
            begin = [64 * b + 32 * owner for b in range(width // 64)]
            runs = jnp.concatenate([value[:, b : b + 32] for b in begin], axis=1)
            hi, lo = split2(runs)
            o_ref[owner, pl.ds(pl.multiple_of(c * columns, columns), columns)] = hi
            o_ref[owner, pl.ds(pl.multiple_of((2 + c) * columns, columns), columns)] = lo


def prep_call(core, own, other):
    columns, n_all = own.shape
    width = 1024
    return pl.pallas_call(
        prep_kernel,
        grid=(n_all // width,),
        out_shape=jax.ShapeDtypeStruct((2, 4 * columns, n_all // 2), BF),
        in_specs=[SMEM] + [pl.BlockSpec((columns, width), lambda g: (0, g))] * 2,
        out_specs=pl.BlockSpec((2, 4 * columns, width // 2), lambda g: (0, 0, g)),
    )(core, own, other)


def main_kernel(chunk, sizes, cols_ref, core_ref, jtab_ref, x_ref, *rest):
    pieces = rest[: len(sizes)]
    carried = rest[len(sizes) : -4]
    give_ref, keep_ref, bt, fc = rest[-4:]
    core = core_ref[0]
    pairs = pieces[0].shape[1]
    n_half, lanes = bt.shape[1:]
    columns = x_ref.shape[1] // 2
    first = core * (cols_ref.shape[0] // 2) + chunk * 2 * pairs

    def zero(r, _):
        s = pl.ds(pl.multiple_of(r * 64, 64), 64)
        bt[0, s] = jnp.zeros((64, lanes), BF)
        bt[1, s] = jnp.zeros((64, lanes), BF)
        return 0

    lax.fori_loop(0, n_half // 64, zero, 0)
    slot = 0
    for piece, size in zip(pieces, sizes):
        for s in range(size):
            j = jtab_ref[slot]
            slot += 1
            for t in range(pairs):
                tile = piece[s, t]
                for h in range(2):
                    row = pl.multiple_of(cols_ref[first + 2 * t + h, j] * 32, 32)
                    lane = t * 128 + h * 64
                    for owner in range(2):
                        part = tile[owner * 32 : owner * 32 + 32, h * 64 : h * 64 + 64]
                        bt[owner, pl.ds(row, 32), lane : lane + 64] = part

    def forward(n, _):
        s = pl.ds(pl.multiple_of(n * 512, 512), 512)
        f = jnp.dot(x_ref[0], bt[0, :, s], preferred_element_type=F32)
        f += jnp.dot(x_ref[1], bt[1, :, s], preferred_element_type=F32)
        hi, lo = split2(f[:columns] + f[columns:])
        fc[0:columns, s] = hi
        fc[columns:, s] = lo
        return 0

    lax.fori_loop(0, lanes // 512, forward, 0)
    groups, _, width = keep_ref.shape
    for place, (out, owner) in enumerate(((give_ref, 1 - core), (keep_ref, core))):

        def backward(n, _, out=out, owner=owner, place=place):
            s = pl.ds(pl.multiple_of(n * 2 * width, 2 * width), 2 * width)
            y = lax.dot_general(
                fc[...], bt[owner, s], (((1,), (1,)), ((), ())), preferred_element_type=F32
            )
            y = y[:columns] + y[columns:]
            for g in range(2):
                part = y[:, g * width : (g + 1) * width]
                if carried:
                    part += carried[place][2 * n + g]
                out[2 * n + g] = part
            return 0

        lax.fori_loop(0, groups // 2, backward, 0)


def main_call(chunk, cols, core, jtab, x, pieces, carried, groups):
    _, columns, n_half = x.shape
    lanes = pieces[0].shape[1] * 128
    sizes = tuple(p.shape[0] for p in pieces)
    shape = jax.ShapeDtypeStruct((groups, columns // 2, n_half // groups), F32)
    flops = 2 * 2 * columns * 2 * n_half * lanes
    return pl.pallas_call(
        functools.partial(main_kernel, chunk, sizes),
        out_shape=(shape, shape),
        in_specs=[SMEM, SMEM, SMEM] + [VMEM] * (1 + len(pieces) + len(carried)),
        out_specs=(VMEM, VMEM),
        scratch_shapes=[pltpu.VMEM((2, n_half, lanes), BF), pltpu.VMEM((columns, lanes), BF)],
        compiler_params=pltpu.CompilerParams(vmem_limit_bytes=48 * 1024 * 1024),
        cost_estimate=pl.CostEstimate(flops=flops, bytes_accessed=16 << 20, transcendentals=0),
    )(cols, core, jtab, x, *pieces, *carried)


def post_kernel(core_ref, w_own_ref, w_other_ref, y_ref, v_ref, own_ref, other_ref, o_ref, loc):
    core = core_ref[0]
    groups = y_ref.shape[0]
    members = w_own_ref.shape[0]
    inner = v_ref.shape[1] // groups
    vhi, vlo = split2(v_ref[...])
    dims = (((1,), (1,)), ((), ()))
    for m in range(2 * members):
        rows = slice(m * inner, (m + 1) * inner)
        column = jnp.concatenate([y_ref[s, rows] for s in range(groups)], axis=0)
        hi, lo = split2(column.T)
        part = lax.dot_general(hi, vhi, dims, preferred_element_type=F32)
        part += lax.dot_general(lo, vhi, dims, preferred_element_type=F32)
        part += lax.dot_general(hi, vlo, dims, preferred_element_type=F32)
        c, k = divmod(m, members)
        loc[c, :, k, :] = part * jnp.where(core == c, w_own_ref[k], w_other_ref[k])
    _, nvar, owned, _ = o_ref.shape
    for d in range(o_ref.shape[0]):
        rows = pl.ds(d * owned, owned)
        near = loc[core, rows]
        far = loc[1 - core, rows]
        for v in range(nvar):
            both = own_ref[d, 0, :, v].astype(F32) * near + other_ref[d, :, v].astype(F32) * far
            o_ref[d, v] = jnp.sum(both, axis=1)


def post_call(core, w_own, w_other, y, v, own, other):
    parts, _, owned, nvar, members, levels = own.shape
    groups, columns, nodes = y.shape
    block = 128
    step = block // owned
    grid_spec = pltpu.PrefetchScalarGridSpec(
        num_scalar_prefetch=1,
        grid=(nodes // block,),
        in_specs=[
            SMEM,
            SMEM,
            pl.BlockSpec((groups, columns, block), lambda g, c: (0, 0, g)),
            pl.BlockSpec((levels, levels), lambda g, c: (0, 0)),
            pl.BlockSpec(
                (step, 1, owned, nvar, members, levels), lambda g, c: (g, c[0], 0, 0, 0, 0)
            ),
            pl.BlockSpec((step, owned, nvar, members, levels), lambda g, c: (g, 0, 0, 0, 0)),
        ],
        out_specs=pl.BlockSpec((step, nvar, owned, levels), lambda g, c: (g, 0, 0, 0)),
        scratch_shapes=[pltpu.VMEM((2, block, members, levels), F32)],
    )
    return pl.pallas_call(
        post_kernel,
        grid_spec=grid_spec,
        out_shape=jax.ShapeDtypeStruct((parts, nvar, owned, levels), F32),
    )(core, w_own, w_other, y, v, own, other)


def gather(unit):
    near = send(unit, Z_NEAR)
    up = send(unit, Y_UP)
    down = send(unit, Y_DOWN)
    far_a = send(up[:1], Y_UP)
    far_b = send(down[1:], Y_DOWN)
    near_up = send(near, Y_UP)
    near_down = send(near, Y_DOWN)
    near_far_a = send(near_up[:1], Y_UP)
    near_far_b = send(near_down[1:], Y_DOWN)
    pieces = [unit, near, up, down, far_a, far_b, near_up, near_down, near_far_a, near_far_b]
    own, other = (0,), (1,)
    both = own + other
    layout = [(0, 0, both), (0, 1, both), (3, 0, both), (1, 0, both), (2, 0, own), (2, 0, other)]
    layout += [(3, 1, both), (1, 1, both), (2, 1, own), (2, 1, other)]
    return pieces, [(dy, dz, dc) for dy, dz, cores in layout for dc in cores]


def slot_table(layout):
    zhi, y, c = lax.axis_index("zhi"), lax.axis_index("y"), lax.axis_index("core")
    dy, dz, dc = (jnp.array(t, jnp.int32) for t in zip(*layout))
    return ((zhi ^ dz) * 8 + ((y + dy) & 3) * 2 + (c ^ dc)).astype(jnp.int32)


def shards(control, perturb, member_weights, blocks, block_cols, vertical):
    nodes_all, mem_dev, lev_dev = control.shape
    members_all = mem_dev * 16
    groups, owned = 8, nodes_all // 128
    core_index = lax.axis_index("core")
    core = core_index.reshape(1).astype(jnp.int32)
    keep, give = pack(core, blocks[:, 0])
    pair = jnp.stack([keep, send(give, CORE)])
    x = control.transpose(1, 2, 0).reshape(mem_dev * lev_dev, nodes_all)
    xc = prep_call(core, x, send(x, CORE))
    weights = member_weights / math.sqrt(members_all - 1)
    weights_other = send(weights, CORE)
    fields = perturb.transpose(0, 2, 1, 3).reshape(8, 2, owned, -1, mem_dev, perturb.shape[3])
    handed = lax.dynamic_index_in_dim(fields, 1 - core_index, 1, keepdims=False)
    fields_other = send(handed, CORE)
    carried = ()
    pairs = pair.shape[1] // CHUNKS
    for chunk in range(CHUNKS):
        pieces, layout = gather(pair[:, chunk * pairs : (chunk + 1) * pairs])
        table = slot_table(layout)
        carried = main_call(chunk, block_cols, core, table, xc, pieces, carried, groups)
    give, keep = carried
    y = keep + send(give, CORE)
    y = lax.all_to_all(y, ("x", "zlo"), split_axis=0, concat_axis=0, tiled=True)
    out = post_call(core, weights, weights_other, y, vertical, fields, fields_other)
    out = lax.all_to_all(out, ("zhi", "y"), split_axis=0, concat_axis=0, tiled=True)
    return jnp.sum(out, axis=0).transpose(1, 0, 2)


def solution(mesh):
    fine = Mesh(mesh.devices.reshape(4, 2, 2, 4, 2), AXES)
    lev, mem = ("x", "zlo"), ("zhi", "y", "core")
    in_specs = (
        P(None, mem, lev),
        P(lev, mem, None, None),
        P(mem),
        P(None, mem, None, None),
        P(),
        P(),
    )
    out_specs = P(AXES, None, None)
    return jax.shard_map(shards, mesh=fine, in_specs=in_specs, out_specs=out_specs, check_vma=False)
```

```python
import functools
import math

import jax
import jax.numpy as jnp
from jax import lax
from jax.experimental import pallas as pl
from jax.experimental.pallas import tpu as pltpu
from jax.sharding import Mesh
from jax.sharding import PartitionSpec as P

BF = jnp.bfloat16
F32 = jnp.float32
AXES = ("x", "zlo", "zhi", "y", "core")
CHUNKS = 2


def coords(d):
    x, zlo, zhi, y, c = d // 32, d // 16 % 2, d // 8 % 2, d // 2 % 4, d % 2
    return x, y, 2 * zhi + zlo, c


def device(x, y, z, c):
    return (x % 4) * 32 + (z % 2) * 16 + (z // 2) * 8 + (y % 4) * 2 + c


def perm(move):
    return [(d, device(*move(*coords(d)))) for d in range(128)]


Z_NEAR = perm(lambda x, y, z, c: (x, y, 3 - z, c))
Y_UP = perm(lambda x, y, z, c: (x, y + 1, z, c))
Y_DOWN = perm(lambda x, y, z, c: (x, y - 1, z, c))
Y_FAR = perm(lambda x, y, z, c: (x, y + 2, z, c))
CORE = perm(lambda x, y, z, c: (x, y, z, 1 - c))
VMEM = pl.BlockSpec(memory_space=pltpu.VMEM)
SMEM = pl.BlockSpec(memory_space=pltpu.SMEM)


def send(value, pairs):
    return lax.ppermute(value, AXES, pairs)


def split2(x):
    hi = x.astype(BF)
    return hi, (x - hi.astype(F32)).astype(BF)


def pack_kernel(core_ref, own_ref, other_ref, *outs):
    rows = outs[0].shape[1]
    for place, out in enumerate(outs):
        first = core_ref[0] * (own_ref.shape[0] // 2) + 2 * rows * place
        for slot, ref in enumerate((own_ref, other_ref)):
            for t in range(rows):
                i = first + 2 * t
                two = jnp.concatenate([ref[i], ref[i + 1]], axis=0).astype(F32)
                out[slot, t] = two.T.astype(BF)


def pack(core, own, other):
    n, p, q = own.shape
    shape = jax.ShapeDtypeStruct((2, n // 4 // CHUNKS, q, 2 * p), BF)
    return pl.pallas_call(
        pack_kernel,
        out_shape=(shape,) * CHUNKS,
        in_specs=[SMEM, VMEM, VMEM],
        out_specs=(VMEM,) * CHUNKS,
    )(core, own, other)


def prep_kernel(core_ref, own_ref, other_ref, o_ref):
    core = core_ref[0]
    columns, width = own_ref.shape
    for ref, c in ((own_ref, core), (other_ref, 1 - core)):
        value = ref[...]
        for owner in range(2):
            begin = [64 * b + 32 * owner for b in range(width // 64)]
            runs = jnp.concatenate([value[:, b : b + 32] for b in begin], axis=1)
            hi, lo = split2(runs)
            o_ref[owner, pl.ds(pl.multiple_of(c * columns, columns), columns)] = hi
            o_ref[owner, pl.ds(pl.multiple_of((2 + c) * columns, columns), columns)] = lo


def prep_call(core, own, other):
    columns, n_all = own.shape
    width = 1024
    return pl.pallas_call(
        prep_kernel,
        grid=(n_all // width,),
        out_shape=jax.ShapeDtypeStruct((2, 4 * columns, n_all // 2), BF),
        in_specs=[SMEM] + [pl.BlockSpec((columns, width), lambda g: (0, g))] * 2,
        out_specs=pl.BlockSpec((2, 4 * columns, width // 2), lambda g: (0, 0, g)),
    )(core, own, other)


def main_kernel(chunk, sizes, cols_ref, core_ref, jtab_ref, x_ref, *rest):
    pieces = rest[: len(sizes)]
    carried = rest[len(sizes) : -4]
    give_ref, keep_ref, bt, fc = rest[-4:]
    core = core_ref[0]
    pairs = pieces[0].shape[1]
    n_half, lanes = bt.shape[1:]
    columns = x_ref.shape[1] // 2
    first = core * (cols_ref.shape[0] // 2) + chunk * 2 * pairs

    def zero(r, _):
        s = pl.ds(pl.multiple_of(r * 64, 64), 64)
        bt[0, s] = jnp.zeros((64, lanes), BF)
        bt[1, s] = jnp.zeros((64, lanes), BF)
        return 0

    lax.fori_loop(0, n_half // 64, zero, 0)
    slot = 0
    for piece, size in zip(pieces, sizes):
        for s in range(size):
            j = jtab_ref[slot]
            slot += 1
            for t in range(pairs):
                tile = piece[s, t]
                for h in range(2):
                    row = pl.multiple_of(cols_ref[first + 2 * t + h, j] * 32, 32)
                    lane = t * 128 + h * 64
                    for owner in range(2):
                        part = tile[owner * 32 : owner * 32 + 32, h * 64 : h * 64 + 64]
                        bt[owner, pl.ds(row, 32), lane : lane + 64] = part

    def forward(n, _):
        s = pl.ds(pl.multiple_of(n * 512, 512), 512)
        f = jnp.dot(x_ref[0], bt[0, :, s], preferred_element_type=F32)
        f += jnp.dot(x_ref[1], bt[1, :, s], preferred_element_type=F32)
        hi, lo = split2(f[:columns] + f[columns:])
        fc[0:columns, s] = hi
        fc[columns:, s] = lo
        return 0

    lax.fori_loop(0, lanes // 512, forward, 0)
    groups, _, width = keep_ref.shape
    for place, (out, owner) in enumerate(((give_ref, 1 - core), (keep_ref, core))):

        def backward(n, _, out=out, owner=owner, place=place):
            s = pl.ds(pl.multiple_of(n * 2 * width, 2 * width), 2 * width)
            y = lax.dot_general(
                fc[...], bt[owner, s], (((1,), (1,)), ((), ())), preferred_element_type=F32
            )
            y = y[:columns] + y[columns:]
            for g in range(2):
                part = y[:, g * width : (g + 1) * width]
                if carried:
                    part += carried[place][2 * n + g]
                out[2 * n + g] = part
            return 0

        lax.fori_loop(0, groups // 2, backward, 0)


def main_call(chunk, cols, core, jtab, x, pieces, carried, groups):
    _, columns, n_half = x.shape
    lanes = pieces[0].shape[1] * 128
    sizes = tuple(p.shape[0] for p in pieces)
    shape = jax.ShapeDtypeStruct((groups, columns // 2, n_half // groups), F32)
    flops = 2 * 2 * columns * 2 * n_half * lanes
    return pl.pallas_call(
        functools.partial(main_kernel, chunk, sizes),
        out_shape=(shape, shape),
        in_specs=[SMEM, SMEM, SMEM] + [VMEM] * (1 + len(pieces) + len(carried)),
        out_specs=(VMEM, VMEM),
        scratch_shapes=[pltpu.VMEM((2, n_half, lanes), BF), pltpu.VMEM((columns, lanes), BF)],
        compiler_params=pltpu.CompilerParams(vmem_limit_bytes=48 * 1024 * 1024),
        cost_estimate=pl.CostEstimate(flops=flops, bytes_accessed=16 << 20, transcendentals=0),
    )(cols, core, jtab, x, *pieces, *carried)


def post_kernel(core_ref, w_own_ref, w_other_ref, y_ref, v_ref, own_ref, other_ref, o_ref, loc):
    core = core_ref[0]
    groups = y_ref.shape[0]
    block = loc.shape[1]
    nodes = pl.ds(pl.multiple_of(pl.program_id(0) * block, block), block)
    members = w_own_ref.shape[0]
    inner = v_ref.shape[1] // groups
    vhi, vlo = split2(v_ref[...])
    dims = (((1,), (1,)), ((), ()))
    for m in range(2 * members):
        rows = slice(m * inner, (m + 1) * inner)
        column = jnp.concatenate([y_ref[s, rows, nodes] for s in range(groups)], axis=0)
        hi, lo = split2(column.T)
        part = lax.dot_general(hi, vhi, dims, preferred_element_type=F32)
        part += lax.dot_general(lo, vhi, dims, preferred_element_type=F32)
        part += lax.dot_general(hi, vlo, dims, preferred_element_type=F32)
        c, k = divmod(m, members)
        loc[c, :, k, :] = part * jnp.where(core == c, w_own_ref[k], w_other_ref[k])
    _, nvar, owned, _ = o_ref.shape
    for d in range(o_ref.shape[0]):
        rows = pl.ds(d * owned, owned)
        near = loc[core, rows]
        far = loc[1 - core, rows]
        for v in range(nvar):
            both = own_ref[d, 0, :, v].astype(F32) * near
            both += other_ref[d, 0, :, v].astype(F32) * far
            o_ref[d, v] = jnp.sum(both, axis=1)


def post_call(core, w_own, w_other, y, v, own, other):
    parts, _, owned, nvar, members, levels = own.shape
    groups, columns, nodes = y.shape
    block = 128
    step = block // owned
    grid_spec = pltpu.PrefetchScalarGridSpec(
        num_scalar_prefetch=1,
        grid=(nodes // block,),
        in_specs=[
            SMEM,
            SMEM,
            VMEM,
            pl.BlockSpec((levels, levels), lambda g, c: (0, 0)),
            pl.BlockSpec(
                (step, 1, owned, nvar, members, levels), lambda g, c: (g, c[0], 0, 0, 0, 0)
            ),
            pl.BlockSpec(
                (step, 1, owned, nvar, members, levels), lambda g, c: (g, c[0], 0, 0, 0, 0)
            ),
        ],
        out_specs=pl.BlockSpec((step, nvar, owned, levels), lambda g, c: (g, 0, 0, 0)),
        scratch_shapes=[pltpu.VMEM((2, block, members, levels), F32)],
    )
    return pl.pallas_call(
        post_kernel,
        grid_spec=grid_spec,
        out_shape=jax.ShapeDtypeStruct((parts, nvar, owned, levels), F32),
    )(core, w_own, w_other, y, v, own, other)


LAYOUT = ((0, 0), (0, 1), (3, 0), (1, 0), (2, 0), (3, 1), (1, 1), (2, 1))


def gather(unit):
    near = send(unit, Z_NEAR)
    up = send(unit, Y_UP)
    down = send(unit, Y_DOWN)
    far = send(unit, Y_FAR)
    near_up = send(near, Y_UP)
    near_down = send(near, Y_DOWN)
    near_far = send(far, Z_NEAR)
    return [unit, near, up, down, far, near_up, near_down, near_far]


def slot_table():
    zhi, y, c = lax.axis_index("zhi"), lax.axis_index("y"), lax.axis_index("core")
    slot = jnp.arange(16, dtype=jnp.int32)
    dy, dz = (sum(jnp.where(slot // 2 == i, d[n], 0) for i, d in enumerate(LAYOUT)) for n in (0, 1))
    return ((zhi ^ dz) * 8 + ((y + dy) & 3) * 2 + (c ^ (slot & 1))).astype(jnp.int32)


def shards(control, perturb, member_weights, blocks, block_cols, vertical):
    nodes_all, mem_dev, lev_dev = control.shape
    members_all = mem_dev * 16
    groups, owned = 8, nodes_all // 128
    core_index = lax.axis_index("core")
    core = core_index.reshape(1).astype(jnp.int32)
    stored = blocks[:, 0]
    units = pack(core, stored, send(stored, CORE))
    x = control.transpose(1, 2, 0).reshape(mem_dev * lev_dev, nodes_all)
    xc = prep_call(core, x, send(x, CORE))
    weights = member_weights / math.sqrt(members_all - 1)
    weights_other = send(weights, CORE)
    fields = perturb.transpose(0, 2, 1, 3)
    fields_other = send(fields, CORE)
    shape = (groups, 2, owned) + fields.shape[1:]
    fields, fields_other = fields.reshape(shape), fields_other.reshape(shape)
    table = slot_table()
    carried = ()
    gathered = [gather(unit) for unit in units]
    for chunk, pieces in enumerate(gathered):
        carried = main_call(chunk, block_cols, core, table, xc, pieces, carried, groups)
    give, keep = carried
    y = keep + send(give, CORE)
    y = lax.all_to_all(y, ("x", "zlo"), split_axis=0, concat_axis=0, tiled=True)
    out = post_call(core, weights, weights_other, y, vertical, fields, fields_other)
    out = lax.all_to_all(out, ("zhi", "y"), split_axis=0, concat_axis=0, tiled=True)
    return jnp.sum(out, axis=0).transpose(1, 0, 2)


def solution(mesh):
    fine = Mesh(mesh.devices.reshape(4, 2, 2, 4, 2), AXES)
    lev, mem = ("x", "zlo"), ("zhi", "y", "core")
    in_specs = (
        P(None, mem, lev),
        P(lev, mem, None, None),
        P(mem),
        P(None, mem, None, None),
        P(),
        P(),
    )
    out_specs = P(AXES, None, None)
    return jax.shard_map(shards, mesh=fine, in_specs=in_specs, out_specs=out_specs, check_vma=False)
```

```python
import functools
import math

import jax
import jax.numpy as jnp
from jax import lax
from jax.experimental import pallas as pl
from jax.experimental.pallas import tpu as pltpu
from jax.sharding import Mesh
from jax.sharding import PartitionSpec as P

BF = jnp.bfloat16
F32 = jnp.float32
AXES = ("x", "zlo", "zhi", "y", "core")


def coords(d):
    x, zlo, zhi, y, c = d // 32, d // 16 % 2, d // 8 % 2, d // 2 % 4, d % 2
    return x, y, 2 * zhi + zlo, c


def device(x, y, z, c):
    return (x % 4) * 32 + (z % 2) * 16 + (z // 2) * 8 + (y % 4) * 2 + c


def perm(move):
    return [(d, device(*move(*coords(d)))) for d in range(128)]


Z_NEAR = perm(lambda x, y, z, c: (x, y, 3 - z, c))
Y_UP = perm(lambda x, y, z, c: (x, y + 1, z, c))
Y_DOWN = perm(lambda x, y, z, c: (x, y - 1, z, c))
Y_FAR = perm(lambda x, y, z, c: (x, y + 2, z, c))
CORE = perm(lambda x, y, z, c: (x, y, z, 1 - c))
LIMIT = 20 * 1024 * 1024
VMEM = pl.BlockSpec(memory_space=pltpu.VMEM)
SMEM = pl.BlockSpec(memory_space=pltpu.SMEM)


def send(value, pairs):
    return lax.ppermute(value, AXES, pairs)


def split2(x):
    hi = x.astype(BF)
    return hi, (x - hi.astype(F32)).astype(BF)


def pack_kernel(half_ref, b_ref, o_ref):
    rows = o_ref.shape[0]
    for t in range(rows):
        i = 2 * (half_ref[0] * rows + t)
        two = jnp.concatenate([b_ref[i], b_ref[i + 1]], axis=0).astype(F32)
        o_ref[t] = two.T.astype(BF)


def pack(half, b):
    n, p, q = b.shape
    return pl.pallas_call(
        pack_kernel,
        out_shape=jax.ShapeDtypeStruct((n // 4, q, 2 * p), BF),
        in_specs=[SMEM, VMEM],
        out_specs=VMEM,
        compiler_params=pltpu.CompilerParams(vmem_limit_bytes=LIMIT),
    )(half, b)


def prep_kernel(core_ref, own_ref, other_ref, o_ref):
    core = core_ref[0]
    columns, width = own_ref.shape
    for ref, c in ((own_ref, core), (other_ref, 1 - core)):
        value = ref[...]
        for owner in range(2):
            begin = [64 * b + 32 * owner for b in range(width // 64)]
            runs = jnp.concatenate([value[:, b : b + 32] for b in begin], axis=1)
            hi, lo = split2(runs)
            o_ref[owner, pl.ds(pl.multiple_of(c * columns, columns), columns)] = hi
            o_ref[owner, pl.ds(pl.multiple_of((2 + c) * columns, columns), columns)] = lo


def prep_call(core, own, other):
    columns, n_all = own.shape
    width = 1024
    return pl.pallas_call(
        prep_kernel,
        grid=(n_all // width,),
        out_shape=jax.ShapeDtypeStruct((2, 4 * columns, n_all // 2), BF),
        in_specs=[SMEM] + [pl.BlockSpec((columns, width), lambda g: (0, g))] * 2,
        out_specs=pl.BlockSpec((2, 4 * columns, width // 2), lambda g: (0, 0, g)),
        compiler_params=pltpu.CompilerParams(vmem_limit_bytes=LIMIT),
    )(core, own, other)


def place_kernel(slots, cols_ref, core_ref, jtab_ref, *rest):
    pieces, bt = rest[: len(slots)], rest[-1]
    n_half, lanes = bt.shape[1:]
    first = core_ref[0] * (cols_ref.shape[0] // 2)
    if len(rest) == len(slots) + 1:

        def zero(r, _):
            s = pl.ds(pl.multiple_of(r * 64, 64), 64)
            bt[0, s] = jnp.zeros((64, lanes), BF)
            bt[1, s] = jnp.zeros((64, lanes), BF)
            return 0

        lax.fori_loop(0, n_half // 64, zero, 0)
    for piece, slot in zip(pieces, slots):
        for s in range(piece.shape[0]):
            j = jtab_ref[slot + s]
            for t in range(piece.shape[1]):
                tile = piece[s, t]
                for h in range(2):
                    row = pl.multiple_of(cols_ref[first + 2 * t + h, j] * 32, 32)
                    lane = t * 128 + h * 64
                    for owner in range(2):
                        part = tile[owner * 32 : owner * 32 + 32, h * 64 : h * 64 + 64]
                        bt[owner, pl.ds(row, 32), lane : lane + 64] = part


def place_call(cols, core, jtab, pieces, slots, shape, dense=None):
    given = () if dense is None else (dense,)
    position = 3 + len(pieces)
    return pl.pallas_call(
        functools.partial(place_kernel, slots),
        out_shape=jax.ShapeDtypeStruct(shape, BF),
        in_specs=[SMEM] * 3 + [VMEM] * (len(pieces) + len(given)),
        out_specs=VMEM,
        input_output_aliases={position: 0} if given else {},
        compiler_params=pltpu.CompilerParams(vmem_limit_bytes=LIMIT),
    )(cols, core, jtab, *pieces, *given)


def forward_kernel(x_ref, bt, f_ref):
    columns = x_ref.shape[1] // 2
    width = 1024

    def step(n, _):
        s = pl.ds(pl.multiple_of(n * width, width), width)
        f = jnp.dot(x_ref[0], bt[0, :, s], preferred_element_type=F32)
        f += jnp.dot(x_ref[1], bt[1, :, s], preferred_element_type=F32)
        hi, lo = split2(f[:columns] + f[columns:])
        f_ref[0:columns, s] = hi
        f_ref[columns:, s] = lo
        return 0

    lax.fori_loop(0, bt.shape[2] // width, step, 0)


def backward_kernel(owner_ref, f_ref, bt, o_ref):
    groups, columns, width = o_ref.shape
    per = 4

    def step(n, _):
        s = pl.ds(pl.multiple_of(n * per * width, per * width), per * width)
        y = lax.dot_general(
            f_ref[...], bt[owner_ref[0], s], (((1,), (1,)), ((), ())), preferred_element_type=F32
        )
        y = y[:columns] + y[columns:]
        for g in range(per):
            o_ref[per * n + g] = y[:, g * width : (g + 1) * width]
        return 0

    lax.fori_loop(0, groups // per, step, 0)


def forward_call(x, dense):
    lanes = dense.shape[2]
    flops = 4 * x.shape[1] * x.shape[2] * lanes
    return pl.pallas_call(
        forward_kernel,
        out_shape=jax.ShapeDtypeStruct((x.shape[1], lanes), BF),
        in_specs=[VMEM, VMEM],
        out_specs=VMEM,
        compiler_params=pltpu.CompilerParams(vmem_limit_bytes=LIMIT),
        cost_estimate=pl.CostEstimate(flops=flops, bytes_accessed=8 << 20, transcendentals=0),
    )(x, dense)


def backward_call(owner, f, dense, groups):
    n_half, lanes = dense.shape[1:]
    flops = 2 * f.shape[0] * n_half * lanes
    return pl.pallas_call(
        backward_kernel,
        out_shape=jax.ShapeDtypeStruct((groups, f.shape[0] // 2, n_half // groups), F32),
        in_specs=[SMEM, VMEM, VMEM],
        out_specs=VMEM,
        compiler_params=pltpu.CompilerParams(vmem_limit_bytes=LIMIT),
        cost_estimate=pl.CostEstimate(flops=flops, bytes_accessed=4 << 20, transcendentals=0),
    )(owner, f, dense)


def post_kernel(core_ref, w_own_ref, w_other_ref, y_ref, v_ref, own_ref, other_ref, o_ref, loc):
    core = core_ref[0]
    groups = y_ref.shape[0]
    block = loc.shape[1]
    nodes = pl.ds(pl.multiple_of(pl.program_id(0) * block, block), block)
    members = w_own_ref.shape[0]
    inner = v_ref.shape[1] // groups
    vhi, vlo = split2(v_ref[...])
    dims = (((1,), (1,)), ((), ()))
    for m in range(2 * members):
        rows = slice(m * inner, (m + 1) * inner)
        column = jnp.concatenate([y_ref[s, rows, nodes] for s in range(groups)], axis=0)
        hi, lo = split2(column.T)
        part = lax.dot_general(hi, vhi, dims, preferred_element_type=F32)
        part += lax.dot_general(lo, vhi, dims, preferred_element_type=F32)
        part += lax.dot_general(hi, vlo, dims, preferred_element_type=F32)
        c, k = divmod(m, members)
        loc[c, :, k, :] = part * jnp.where(core == c, w_own_ref[k], w_other_ref[k])
    _, nvar, owned, _ = o_ref.shape
    for d in range(o_ref.shape[0]):
        rows = pl.ds(d * owned, owned)
        near = loc[core, rows]
        far = loc[1 - core, rows]
        for v in range(nvar):
            both = own_ref[d, 0, :, v].astype(F32) * near
            both += other_ref[d, 0, :, v].astype(F32) * far
            o_ref[d, v] = jnp.sum(both, axis=1)


def post_call(core, w_own, w_other, y, v, own, other):
    parts, _, owned, nvar, members, levels = own.shape
    _, _, nodes = y.shape
    block = 128
    step = block // owned
    grid_spec = pltpu.PrefetchScalarGridSpec(
        num_scalar_prefetch=1,
        grid=(nodes // block,),
        in_specs=[
            SMEM,
            SMEM,
            VMEM,
            pl.BlockSpec((levels, levels), lambda g, c: (0, 0)),
            pl.BlockSpec(
                (step, 1, owned, nvar, members, levels), lambda g, c: (g, c[0], 0, 0, 0, 0)
            ),
            pl.BlockSpec(
                (step, 1, owned, nvar, members, levels), lambda g, c: (g, c[0], 0, 0, 0, 0)
            ),
        ],
        out_specs=pl.BlockSpec((step, nvar, owned, levels), lambda g, c: (g, 0, 0, 0)),
        scratch_shapes=[pltpu.VMEM((2, block, members, levels), F32)],
    )
    return pl.pallas_call(
        post_kernel,
        grid_spec=grid_spec,
        out_shape=jax.ShapeDtypeStruct((parts, nvar, owned, levels), F32),
        compiler_params=pltpu.CompilerParams(vmem_limit_bytes=LIMIT),
    )(core, w_own, w_other, y, v, own, other)


LAYOUT = ((0, 0), (0, 1), (3, 0), (1, 0), (2, 0), (3, 1), (1, 1), (2, 1))


STAGES = ((0,), (1, 2, 3), (4,), (5, 6, 7))


def gather(unit):
    near = send(unit, Z_NEAR)
    up = send(unit, Y_UP)
    down = send(unit, Y_DOWN)
    far = send(unit, Y_FAR)
    near_up = send(near, Y_UP)
    near_down = send(near, Y_DOWN)
    near_far = send(far, Z_NEAR)
    return [unit, near, up, down, far, near_up, near_down, near_far]


def slot_table():
    zhi, y, c = lax.axis_index("zhi"), lax.axis_index("y"), lax.axis_index("core")
    slot = jnp.arange(16, dtype=jnp.int32)
    dy, dz = (sum(jnp.where(slot // 2 == i, d[n], 0) for i, d in enumerate(LAYOUT)) for n in (0, 1))
    return ((zhi ^ dz) * 8 + ((y + dy) & 3) * 2 + (c ^ (slot & 1))).astype(jnp.int32)


def shards(control, perturb, member_weights, blocks, block_cols, vertical):
    nodes_all, mem_dev, lev_dev = control.shape
    members_all = mem_dev * 16
    groups, owned = 8, nodes_all // 128
    core_index = lax.axis_index("core")
    core = core_index.reshape(1).astype(jnp.int32)
    other = 1 - core
    stored = blocks[:, 0]
    handed = send(pack(other, stored), CORE)
    pieces = gather(jnp.stack([pack(core, stored), handed]))
    x = control.transpose(1, 2, 0).reshape(mem_dev * lev_dev, nodes_all)
    x_other = send(x, CORE)
    xc = prep_call(core, x, x_other)
    weights = member_weights / math.sqrt(members_all - 1)
    weights_other = send(weights, CORE)
    fields = perturb.transpose(0, 2, 1, 3)
    fields_other = send(fields, CORE)
    shape = (groups, 2, owned) + fields.shape[1:]
    fields, fields_other = fields.reshape(shape), fields_other.reshape(shape)
    table = slot_table()
    shape = (2, nodes_all // 2, nodes_all // 2)
    dense = None
    for part in STAGES:
        slots = tuple(2 * p for p in part)
        some = [pieces[p] for p in part]
        dense = place_call(block_cols, core, table, some, slots, shape, dense)
    f = forward_call(xc, dense)
    give = backward_call(other, f, dense, groups)
    keep = backward_call(core, f, dense, groups)
    y = keep + send(give, CORE)
    y = lax.all_to_all(y, ("x", "zlo"), split_axis=0, concat_axis=0, tiled=True)
    out = post_call(core, weights, weights_other, y, vertical, fields, fields_other)
    out = lax.all_to_all(out, ("zhi", "y"), split_axis=0, concat_axis=0, tiled=True)
    return jnp.sum(out, axis=0).transpose(1, 0, 2)


def solution(mesh):
    fine = Mesh(mesh.devices.reshape(4, 2, 2, 4, 2), AXES)
    lev, mem = ("x", "zlo"), ("zhi", "y", "core")
    in_specs = (
        P(None, mem, lev),
        P(lev, mem, None, None),
        P(mem),
        P(None, mem, None, None),
        P(),
        P(),
    )
    out_specs = P(AXES, None, None)

    return jax.shard_map(shards, mesh=fine, in_specs=in_specs, out_specs=out_specs, check_vma=False)
```

```python
import functools
import math

import jax
import jax.numpy as jnp
from jax import lax
from jax.experimental import pallas as pl
from jax.experimental.pallas import tpu as pltpu
from jax.sharding import Mesh
from jax.sharding import PartitionSpec as P

BF = jnp.bfloat16
F32 = jnp.float32
AXES = ("x", "zlo", "zhi", "y", "core")


def coords(d):
    x, zlo, zhi, y, c = d // 32, d // 16 % 2, d // 8 % 2, d // 2 % 4, d % 2
    return x, y, 2 * zhi + zlo, c


def device(x, y, z, c):
    return (x % 4) * 32 + (z % 2) * 16 + (z // 2) * 8 + (y % 4) * 2 + c


def perm(move):
    return [(d, device(*move(*coords(d)))) for d in range(128)]


Z_NEAR = perm(lambda x, y, z, c: (x, y, 3 - z, c))
Y_UP = perm(lambda x, y, z, c: (x, y + 1, z, c))
Y_DOWN = perm(lambda x, y, z, c: (x, y - 1, z, c))
Y_FAR = perm(lambda x, y, z, c: (x, y + 2, z, c))
X_PAIR = perm(lambda x, y, z, c: (x ^ 1, y, z, c))
CORE = perm(lambda x, y, z, c: (x, y, z, 1 - c))
LIMIT = 20 * 1024 * 1024
VMEM = pl.BlockSpec(memory_space=pltpu.VMEM)
SMEM = pl.BlockSpec(memory_space=pltpu.SMEM)


def send(value, pairs):
    return lax.ppermute(value, AXES, pairs)


def split2(x):
    hi = x.astype(BF)
    return hi, (x - hi.astype(F32)).astype(BF)


def pack_kernel(half_ref, b_ref, o_ref):
    rows = o_ref.shape[0]
    for t in range(rows):
        i = 2 * (half_ref[0] * rows + t)
        two = jnp.concatenate([b_ref[i], b_ref[i + 1]], axis=0).astype(F32)
        o_ref[t] = two.T.astype(BF)


def pack(half, b):
    n, p, q = b.shape
    return pl.pallas_call(
        pack_kernel,
        out_shape=jax.ShapeDtypeStruct((n // 4, q, 2 * p), BF),
        in_specs=[SMEM, VMEM],
        out_specs=VMEM,
        compiler_params=pltpu.CompilerParams(vmem_limit_bytes=LIMIT),
    )(half, b)


def assemble_kernel(odd_ref, keep_ref, handed_ref, unit_ref, first_ref, second_ref, far_ref):
    half = first_ref.shape[1]
    for slot, ref in enumerate((keep_ref, handed_ref)):
        unit_ref[slot] = ref[...]
        first_ref[slot] = ref[:half]
        second_ref[slot] = ref[half:]

        @pl.when(odd_ref[0] == slot)
        def _(ref=ref):
            far_ref[0] = ref[...]


def assemble(odd, keep, handed):
    rows, q, p = keep.shape
    counts = ((2, rows), (2, rows // 2), (2, rows // 2), (1, rows))
    return pl.pallas_call(
        assemble_kernel,
        out_shape=tuple(jax.ShapeDtypeStruct(c + (q, p), BF) for c in counts),
        in_specs=[SMEM, VMEM, VMEM],
        out_specs=(VMEM,) * 4,
        compiler_params=pltpu.CompilerParams(vmem_limit_bytes=LIMIT),
    )(odd, keep, handed)


def prep_kernel(core_ref, own_ref, other_ref, o_ref):
    core = core_ref[0]
    columns, width = own_ref.shape
    for ref, c in ((own_ref, core), (other_ref, 1 - core)):
        value = ref[...]
        for owner in range(2):
            begin = [64 * b + 32 * owner for b in range(width // 64)]
            runs = jnp.concatenate([value[:, b : b + 32] for b in begin], axis=1)
            hi, lo = split2(runs)
            o_ref[owner, pl.ds(pl.multiple_of(c * columns, columns), columns)] = hi
            o_ref[owner, pl.ds(pl.multiple_of((2 + c) * columns, columns), columns)] = lo


def prep_call(core, own, other):
    columns, n_all = own.shape
    width = 1024
    return pl.pallas_call(
        prep_kernel,
        grid=(n_all // width,),
        out_shape=jax.ShapeDtypeStruct((2, 4 * columns, n_all // 2), BF),
        in_specs=[SMEM] + [pl.BlockSpec((columns, width), lambda g: (0, g))] * 2,
        out_specs=pl.BlockSpec((2, 4 * columns, width // 2), lambda g: (0, 0, g)),
        compiler_params=pltpu.CompilerParams(vmem_limit_bytes=LIMIT),
    )(core, own, other)


def place_kernel(plan, zero_first, cols_ref, core_ref, jtab_ref, *rest):
    pieces, bt = rest[: len(plan)], rest[-1]
    n_half, lanes = bt.shape[1:]
    first = core_ref[0] * (cols_ref.shape[0] // 2)
    if zero_first:

        def zero(r, _):
            s = pl.ds(pl.multiple_of(r * 64, 64), 64)
            bt[0, s] = jnp.zeros((64, lanes), BF)
            bt[1, s] = jnp.zeros((64, lanes), BF)
            return 0

        lax.fori_loop(0, n_half // 64, zero, 0)
    for piece, (slot, start) in zip(pieces, plan):
        for s in range(piece.shape[0]):
            j = jtab_ref[slot + s]
            for t in range(piece.shape[1]):
                tile = piece[s, t]
                for h in range(2):
                    i = 2 * (start + t) + h
                    row = pl.multiple_of(cols_ref[first + i, j] * 32, 32)
                    for owner in range(2):
                        part = tile[owner * 32 : owner * 32 + 32, h * 64 : h * 64 + 64]
                        bt[owner, pl.ds(row, 32), i * 64 : i * 64 + 64] = part


def place_call(cols, core, jtab, pieces, plan, shape, dense=None, after=()):
    given = () if dense is None else (dense,)
    position = 3 + len(pieces) + len(after)
    return pl.pallas_call(
        functools.partial(place_kernel, plan, dense is None),
        out_shape=jax.ShapeDtypeStruct(shape, BF),
        in_specs=[SMEM] * 3
        + [VMEM] * len(pieces)
        + [pl.BlockSpec(memory_space=pl.ANY)] * len(after)
        + [VMEM] * len(given),
        out_specs=VMEM,
        input_output_aliases={position: 0} if given else {},
        compiler_params=pltpu.CompilerParams(vmem_limit_bytes=LIMIT),
    )(cols, core, jtab, *pieces, *after, *given)


def forward_kernel(begin, x_ref, bt, f_ref):
    columns = x_ref.shape[1] // 2
    s = slice(begin, begin + f_ref.shape[1])
    f = jnp.dot(x_ref[0], bt[0, :, s], preferred_element_type=F32)
    f += jnp.dot(x_ref[1], bt[1, :, s], preferred_element_type=F32)
    hi, lo = split2(f[:columns] + f[columns:])
    f_ref[0:columns] = hi
    f_ref[columns:] = lo


def backward_kernel(owner_ref, fa_ref, fb_ref, bt, o_ref):
    groups, columns, width = o_ref.shape
    per = 4
    cut = fa_ref.shape[1]
    dims = (((1,), (1,)), ((), ()))

    def step(n, _):
        s = pl.ds(pl.multiple_of(n * per * width, per * width), per * width)
        rows = bt.at[owner_ref[0], s]
        y = lax.dot_general(fa_ref[...], rows[:, :cut], dims, preferred_element_type=F32)
        y += lax.dot_general(fb_ref[...], rows[:, cut:], dims, preferred_element_type=F32)
        y = y[:columns] + y[columns:]
        for g in range(per):
            o_ref[per * n + g] = y[:, g * width : (g + 1) * width]
        return 0

    lax.fori_loop(0, groups // per, step, 0)


def forward_call(x, dense, begin):
    lanes = dense.shape[2] // 2
    flops = 4 * x.shape[1] * x.shape[2] * lanes
    return pl.pallas_call(
        functools.partial(forward_kernel, begin),
        out_shape=jax.ShapeDtypeStruct((x.shape[1], lanes), BF),
        in_specs=[VMEM, VMEM],
        out_specs=VMEM,
        compiler_params=pltpu.CompilerParams(vmem_limit_bytes=LIMIT),
        cost_estimate=pl.CostEstimate(flops=flops, bytes_accessed=8 << 20, transcendentals=0),
    )(x, dense)


def backward_call(owner, fa, fb, dense, groups):
    n_half, lanes = dense.shape[1:]
    flops = 2 * fa.shape[0] * n_half * lanes
    return pl.pallas_call(
        backward_kernel,
        out_shape=jax.ShapeDtypeStruct((groups, fa.shape[0] // 2, n_half // groups), F32),
        in_specs=[SMEM, VMEM, VMEM, VMEM],
        out_specs=VMEM,
        compiler_params=pltpu.CompilerParams(vmem_limit_bytes=LIMIT),
        cost_estimate=pl.CostEstimate(flops=flops, bytes_accessed=4 << 20, transcendentals=0),
    )(owner, fa, fb, dense)


def post_kernel(core_ref, w_own_ref, w_other_ref, y_ref, v_ref, own_ref, other_ref, o_ref, loc):
    core = core_ref[0]
    groups = y_ref.shape[0]
    block = loc.shape[1]
    nodes = pl.ds(pl.multiple_of(pl.program_id(0) * block, block), block)
    members = w_own_ref.shape[0]
    inner = v_ref.shape[1] // groups
    vhi, vlo = split2(v_ref[...])
    dims = (((1,), (1,)), ((), ()))
    for m in range(2 * members):
        rows = slice(m * inner, (m + 1) * inner)
        column = jnp.concatenate([y_ref[s, rows, nodes] for s in range(groups)], axis=0)
        hi, lo = split2(column.T)
        part = lax.dot_general(hi, vhi, dims, preferred_element_type=F32)
        part += lax.dot_general(lo, vhi, dims, preferred_element_type=F32)
        part += lax.dot_general(hi, vlo, dims, preferred_element_type=F32)
        c, k = divmod(m, members)
        loc[c, :, k, :] = part * jnp.where(core == c, w_own_ref[k], w_other_ref[k])
    _, nvar, owned, _ = o_ref.shape
    for d in range(o_ref.shape[0]):
        rows = pl.ds(d * owned, owned)
        near = loc[core, rows]
        far = loc[1 - core, rows]
        for v in range(nvar):
            both = own_ref[d, 0, :, v].astype(F32) * near
            both += other_ref[d, 0, :, v].astype(F32) * far
            o_ref[d, v] = jnp.sum(both, axis=1)


def post_call(core, w_own, w_other, y, v, own, other):
    parts, _, owned, nvar, members, levels = own.shape
    _, _, nodes = y.shape
    block = 128
    step = block // owned
    grid_spec = pltpu.PrefetchScalarGridSpec(
        num_scalar_prefetch=1,
        grid=(nodes // block,),
        in_specs=[
            SMEM,
            SMEM,
            VMEM,
            pl.BlockSpec((levels, levels), lambda g, c: (0, 0)),
            pl.BlockSpec(
                (step, 1, owned, nvar, members, levels), lambda g, c: (g, c[0], 0, 0, 0, 0)
            ),
            pl.BlockSpec(
                (step, 1, owned, nvar, members, levels), lambda g, c: (g, c[0], 0, 0, 0, 0)
            ),
        ],
        out_specs=pl.BlockSpec((step, nvar, owned, levels), lambda g, c: (g, 0, 0, 0)),
        scratch_shapes=[pltpu.VMEM((2, block, members, levels), F32)],
    )
    return pl.pallas_call(
        post_kernel,
        grid_spec=grid_spec,
        out_shape=jax.ShapeDtypeStruct((parts, nvar, owned, levels), F32),
        compiler_params=pltpu.CompilerParams(vmem_limit_bytes=LIMIT),
    )(core, w_own, w_other, y, v, own, other)


SLOTS = (
    [(0, 0, c, 0) for c in (0, 1)]
    + [(0, 1, c, 0) for c in (0, 1)]
    + [(3, 0, c, 0) for c in (0, 1)]
    + [(1, 0, c, 0) for c in (0, 1)]
    + [(2, 0, 0, 1), (2, 0, 1, 1), (2, 1, 0, 1), (2, 1, 1, 1)]
    + [(3, 1, c, 0) for c in (0, 1)]
    + [(1, 1, c, 0) for c in (0, 1)]
)


def gather(keep, handed):
    half = keep.shape[0] // 2
    odd = (lax.axis_index("x") % 2).reshape(1).astype(jnp.int32)
    unit, first, second, chosen = assemble(odd, keep, handed)
    near_a = send(first, Z_NEAR)
    near_b = send(second, Z_NEAR)
    far_a = send(chosen, Y_FAR)
    up = send(unit, Y_UP)
    down = send(unit, Y_DOWN)
    far_b = send(far_a, X_PAIR)
    near_far_a = send(far_a, Z_NEAR)
    up_a = send(near_a, Y_UP)
    down_a = send(near_a, Y_DOWN)
    near_far_b = send(far_b, Z_NEAR)
    up_b = send(near_b, Y_UP)
    down_b = send(near_b, Y_DOWN)
    return (
        ((unit, 0, 0),),
        ((near_a, 2, 0), (near_b, 2, half), (far_a, 8, 0), (far_b, 9, 0)),
        ((up, 4, 0), (down, 6, 0)),
        ((near_far_a, 10, 0), (near_far_b, 11, 0)),
        ((up_a, 12, 0), (down_a, 14, 0)),
        ((up_b, 12, half), (down_b, 14, half)),
    )


def slot_table():
    zhi, y, c = lax.axis_index("zhi"), lax.axis_index("y"), lax.axis_index("core")
    odd = lax.axis_index("x") & 1
    slot = jnp.arange(len(SLOTS), dtype=jnp.int32)
    picks = (sum(jnp.where(slot == i, d[n], 0) for i, d in enumerate(SLOTS)) for n in range(4))
    dy, dz, dc, dx = picks
    return ((zhi ^ dz) * 8 + ((y + dy) & 3) * 2 + (c ^ dc ^ (dx & odd))).astype(jnp.int32)


def shards(control, perturb, member_weights, blocks, block_cols, vertical):
    nodes_all, mem_dev, lev_dev = control.shape
    members_all = mem_dev * 16
    groups, owned = 8, nodes_all // 128
    core_index = lax.axis_index("core")
    core = core_index.reshape(1).astype(jnp.int32)
    other = 1 - core
    stored = blocks[:, 0]
    handed = send(pack(other, stored), CORE)
    stages = gather(pack(core, stored), handed)
    x = control.transpose(1, 2, 0).reshape(mem_dev * lev_dev, nodes_all)
    x_other = send(x, CORE)
    xc = prep_call(core, x, x_other)
    weights = member_weights / math.sqrt(members_all - 1)
    weights_other = send(weights, CORE)
    fields = perturb.transpose(0, 2, 1, 3)
    fields_other = send(fields, CORE)
    shape = (groups, 2, owned) + fields.shape[1:]
    fields, fields_other = fields.reshape(shape), fields_other.reshape(shape)
    table = slot_table()
    shape = (2, nodes_all // 2, nodes_all // 2)
    dense, halves = None, ()
    for stage, parts in enumerate(stages):
        pieces, plan = [p[0] for p in parts], tuple(p[1:] for p in parts)
        args = (block_cols, core, table, pieces, plan, shape)
        dense = place_call(*args, dense, halves)
        if stage >= len(stages) - 2:
            halves += (forward_call(xc, dense, len(halves) * shape[2] // 2),)
    give = backward_call(other, *halves, dense, groups)
    keep = backward_call(core, *halves, dense, groups)
    y = keep + send(give, CORE)
    y = lax.all_to_all(y, ("x", "zlo"), split_axis=0, concat_axis=0, tiled=True)
    out = post_call(core, weights, weights_other, y, vertical, fields, fields_other)
    out = lax.all_to_all(out, ("zhi", "y"), split_axis=0, concat_axis=0, tiled=True)
    return jnp.sum(out, axis=0).transpose(1, 0, 2)


def solution(mesh):
    fine = Mesh(mesh.devices.reshape(4, 2, 2, 4, 2), AXES)
    lev, mem = ("x", "zlo"), ("zhi", "y", "core")
    in_specs = (
        P(None, mem, lev),
        P(lev, mem, None, None),
        P(mem),
        P(None, mem, None, None),
        P(),
        P(),
    )
    out_specs = P(AXES, None, None)

    return jax.shard_map(shards, mesh=fine, in_specs=in_specs, out_specs=out_specs, check_vma=False)
```

```python
import functools
import math

import jax
import jax.numpy as jnp
from jax import lax
from jax.experimental import pallas as pl
from jax.experimental.pallas import tpu as pltpu
from jax.sharding import Mesh
from jax.sharding import PartitionSpec as P

BF = jnp.bfloat16
F32 = jnp.float32
AXES = ("x", "zlo", "zhi", "y", "core")


def coords(d):
    x, zlo, zhi, y, c = d // 32, d // 16 % 2, d // 8 % 2, d // 2 % 4, d % 2
    return x, y, 2 * zhi + zlo, c


def device(x, y, z, c):
    return (x % 4) * 32 + (z % 2) * 16 + (z // 2) * 8 + (y % 4) * 2 + c


def perm(move):
    return [(d, device(*move(*coords(d)))) for d in range(128)]


Z_NEAR = perm(lambda x, y, z, c: (x, y, 3 - z, c))
Y_UP = perm(lambda x, y, z, c: (x, y + 1, z, c))
Y_DOWN = perm(lambda x, y, z, c: (x, y - 1, z, c))
Y_FAR = perm(lambda x, y, z, c: (x, y + 2, z, c))
X_PAIR = perm(lambda x, y, z, c: (x ^ 1, y, z, c))
REACH = ((0, 1), (1, 0), (3, 0), (1, 1), (3, 1), (2, 0), (2, 1), (0, 0))
LEVELS = tuple(
    perm(lambda x, y, z, c, dx=dx, dz=dz: (x + dx, y, z ^ dz, c)) for dx, dz in REACH
)
CUT = 4
CORE = perm(lambda x, y, z, c: (x, y, z, 1 - c))
LIMIT = 20 * 1024 * 1024
VMEM = pl.BlockSpec(memory_space=pltpu.VMEM)
SMEM = pl.BlockSpec(memory_space=pltpu.SMEM)


def send(value, pairs):
    return lax.ppermute(value, AXES, pairs)


def split2(x):
    hi = x.astype(BF)
    return hi, (x - hi.astype(F32)).astype(BF)


def pack_kernel(half_ref, b_ref, o_ref):
    rows = o_ref.shape[0]
    for t in range(rows):
        i = 2 * (half_ref[0] * rows + t)
        two = jnp.concatenate([b_ref[i], b_ref[i + 1]], axis=0).astype(F32)
        o_ref[t] = two.T.astype(BF)


def pack(half, b):
    n, p, q = b.shape
    return pl.pallas_call(
        pack_kernel,
        out_shape=jax.ShapeDtypeStruct((n // 4, q, 2 * p), BF),
        in_specs=[SMEM, VMEM],
        out_specs=VMEM,
        compiler_params=pltpu.CompilerParams(vmem_limit_bytes=LIMIT),
    )(half, b)


def assemble_kernel(odd_ref, keep_ref, handed_ref, unit_ref, first_ref, second_ref, far_ref):
    half = first_ref.shape[1]
    for slot, ref in enumerate((keep_ref, handed_ref)):
        unit_ref[slot] = ref[...]
        first_ref[slot] = ref[:half]
        second_ref[slot] = ref[half:]

        @pl.when(odd_ref[0] == slot)
        def _(ref=ref):
            far_ref[0] = ref[...]


def assemble(odd, keep, handed):
    rows, q, p = keep.shape
    counts = ((2, rows), (2, rows // 2), (2, rows // 2), (1, rows))
    return pl.pallas_call(
        assemble_kernel,
        out_shape=tuple(jax.ShapeDtypeStruct(c + (q, p), BF) for c in counts),
        in_specs=[SMEM, VMEM, VMEM],
        out_specs=(VMEM,) * 4,
        compiler_params=pltpu.CompilerParams(vmem_limit_bytes=LIMIT),
    )(odd, keep, handed)


def prep_kernel(core_ref, own_ref, other_ref, o_ref):
    core = core_ref[0]
    columns, width = own_ref.shape
    for ref, c in ((own_ref, core), (other_ref, 1 - core)):
        value = ref[...]
        for owner in range(2):
            begin = [64 * b + 32 * owner for b in range(width // 64)]
            runs = jnp.concatenate([value[:, b : b + 32] for b in begin], axis=1)
            hi, lo = split2(runs)
            o_ref[owner, pl.ds(pl.multiple_of(c * columns, columns), columns)] = hi
            o_ref[owner, pl.ds(pl.multiple_of((2 + c) * columns, columns), columns)] = lo


def prep_call(core, own, other):
    columns, n_all = own.shape
    width = 1024
    return pl.pallas_call(
        prep_kernel,
        grid=(n_all // width,),
        out_shape=jax.ShapeDtypeStruct((2, 4 * columns, n_all // 2), BF),
        in_specs=[SMEM] + [pl.BlockSpec((columns, width), lambda g: (0, g))] * 2,
        out_specs=pl.BlockSpec((2, 4 * columns, width // 2), lambda g: (0, 0, g)),
        compiler_params=pltpu.CompilerParams(vmem_limit_bytes=LIMIT),
    )(core, own, other)


def place_kernel(plan, zero_first, cols_ref, core_ref, jtab_ref, gx_ref, gz_ref, *rest):
    pieces, bt = rest[: len(plan)], rest[-1]
    n_half, lanes = bt.shape[1:]
    first = core_ref[0] * (cols_ref.shape[0] // 2)
    if zero_first:

        def zero(r, _):
            s = pl.ds(pl.multiple_of(r * 64, 64), 64)
            bt[0, s] = jnp.zeros((64, lanes), BF)
            bt[1, s] = jnp.zeros((64, lanes), BF)
            return 0

        lax.fori_loop(0, n_half // 64, zero, 0)
    for piece, (slot, start) in zip(pieces, plan):
        for s in range(piece.shape[0]):
            j = jtab_ref[slot + s]
            for t in range(piece.shape[1]):
                tile = piece[s, t]
                for h in range(2):
                    i = 2 * (start + t) + h
                    row = pl.multiple_of(cols_ref[first + i, j] * 32, 32)
                    for owner in range(2):
                        part = tile[owner * 32 : owner * 32 + 32, h * 64 : h * 64 + 64]
                        bt[owner, pl.ds(row, 32), i * 64 : i * 64 + 64] = part


def place_call(cols, core, jtab, gx, gz, pieces, plan, shape, dense=None, after=()):
    given = () if dense is None else (dense,)
    position = 5 + len(pieces) + len(after)
    return pl.pallas_call(
        functools.partial(place_kernel, plan, dense is None),
        out_shape=jax.ShapeDtypeStruct(shape, BF),
        in_specs=[SMEM] * 5
        + [VMEM] * len(pieces)
        + [pl.BlockSpec(memory_space=pl.ANY)] * len(after)
        + [VMEM] * len(given),
        out_specs=VMEM,
        input_output_aliases={position: 0} if given else {},
        compiler_params=pltpu.CompilerParams(vmem_limit_bytes=LIMIT),
    )(cols, core, jtab, gx, gz, *pieces, *after, *given)


def forward_kernel(begin, x_ref, bt, f_ref):
    columns = x_ref.shape[1] // 2
    s = slice(begin, begin + f_ref.shape[1])
    f = jnp.dot(x_ref[0], bt[0, :, s], preferred_element_type=F32)
    f += jnp.dot(x_ref[1], bt[1, :, s], preferred_element_type=F32)
    hi, lo = split2(f[:columns] + f[columns:])
    f_ref[0:columns] = hi
    f_ref[columns:] = lo


def backward_kernel(reach, adds, skips, owner_ref, gx_ref, gz_ref, fa_ref, fb_ref, bt, *rest):
    columns = fa_ref.shape[0] // 2
    outs = rest[adds + skips :]
    width = outs[0].shape[-1]
    cut = fa_ref.shape[1]
    dims = (((1,), (1,)), ((), ()))
    for g, (dx, dz) in enumerate(reach):
        group = ((gx_ref[0] + dx) & 3) * 2 + (gz_ref[0] ^ dz)
        s = pl.ds(pl.multiple_of(group * width, width), width)
        rows = bt.at[owner_ref[0], s]
        y = lax.dot_general(fa_ref[...], rows[:, :cut], dims, preferred_element_type=F32)
        y += lax.dot_general(fb_ref[...], rows[:, cut:], dims, preferred_element_type=F32)
        y = y[:columns] + y[columns:]
        if adds:
            outs[g][...] = y + rest[0][g]
        else:
            outs[0][g] = y


def forward_call(x, dense, begin):
    lanes = dense.shape[2] // 2
    flops = 4 * x.shape[1] * x.shape[2] * lanes
    return pl.pallas_call(
        functools.partial(forward_kernel, begin),
        out_shape=jax.ShapeDtypeStruct((x.shape[1], lanes), BF),
        in_specs=[VMEM, VMEM],
        out_specs=VMEM,
        compiler_params=pltpu.CompilerParams(vmem_limit_bytes=LIMIT),
        cost_estimate=pl.CostEstimate(flops=flops, bytes_accessed=8 << 20, transcendentals=0),
    )(x, dense)


def backward_call(owner, gx, gz, reach, fa, fb, dense, added=(), after=()):
    n_half, lanes = dense.shape[1:]
    count = len(reach)
    one = (fa.shape[0] // 2, n_half // 8)
    flops = 2 * fa.shape[0] * n_half * lanes * count // 8
    if added:
        out_shape = (jax.ShapeDtypeStruct(one, F32),) * count
    else:
        out_shape = jax.ShapeDtypeStruct((count,) + one, F32)
    return pl.pallas_call(
        functools.partial(backward_kernel, reach, len(added), len(after)),
        out_shape=out_shape,
        in_specs=[SMEM] * 3
        + [VMEM] * (3 + len(added))
        + [pl.BlockSpec(memory_space=pl.ANY)] * len(after),
        out_specs=(VMEM,) * count if added else VMEM,
        compiler_params=pltpu.CompilerParams(vmem_limit_bytes=LIMIT),
        cost_estimate=pl.CostEstimate(flops=flops, bytes_accessed=4 << 20, transcendentals=0),
    )(owner, gx, gz, fa, fb, dense, *added, *after)


def post_kernel(core_ref, w_own_ref, w_other_ref, gx_ref, gz_ref, v_ref, own_ref, other_ref, *rest):
    sources, (o_ref, loc, vt) = rest[:-3], rest[-3:]
    core = core_ref[0]
    groups = len(sources)
    block = loc.shape[1]
    nodes = pl.ds(pl.multiple_of(pl.program_id(0) * block, block), block)
    members = w_own_ref.shape[0]
    inner = v_ref.shape[1] // groups
    vt[...] = v_ref[...].T
    came = [((gx_ref[0] - dx) & 3) * 2 + (gz_ref[0] ^ dz) for dx, dz in REACH]
    begin = [pl.multiple_of(lev * inner, inner) for lev in came]
    vhi, vlo = split2(jnp.concatenate([vt[pl.ds(b, inner)] for b in begin], axis=0))
    for m in range(2 * members):
        rows = slice(m * inner, (m + 1) * inner)
        column = jnp.concatenate([source[rows, nodes] for source in sources], axis=0)
        hi, lo = split2(column.T)
        part = jnp.dot(hi, vhi, preferred_element_type=F32)
        part += jnp.dot(lo, vhi, preferred_element_type=F32)
        part += jnp.dot(hi, vlo, preferred_element_type=F32)
        c, k = divmod(m, members)
        loc[c, :, k, :] = part * jnp.where(core == c, w_own_ref[k], w_other_ref[k])
    _, nvar, owned, _ = o_ref.shape
    for d in range(o_ref.shape[0]):
        rows = pl.ds(d * owned, owned)
        near = loc[core, rows]
        far = loc[1 - core, rows]
        for v in range(nvar):
            both = own_ref[d, 0, :, v].astype(F32) * near
            both += other_ref[d, 0, :, v].astype(F32) * far
            o_ref[d, v] = jnp.sum(both, axis=1)


def post_call(core, w_own, w_other, gx, gz, v, own, other, sources):
    parts, _, owned, nvar, members, levels = own.shape
    nodes = sources[0].shape[1]
    block = 128
    step = block // owned
    field = pl.BlockSpec(
        (step, 1, owned, nvar, members, levels), lambda g, c: (g, c[0], 0, 0, 0, 0)
    )
    grid_spec = pltpu.PrefetchScalarGridSpec(
        num_scalar_prefetch=1,
        grid=(nodes // block,),
        in_specs=[SMEM] * 4
        + [pl.BlockSpec((levels, levels), lambda g, c: (0, 0)), field, field]
        + [VMEM] * len(sources),
        out_specs=pl.BlockSpec((step, nvar, owned, levels), lambda g, c: (g, 0, 0, 0)),
        scratch_shapes=[
            pltpu.VMEM((2, block, members, levels), F32),
            pltpu.VMEM((levels, levels), F32),
        ],
    )
    return pl.pallas_call(
        post_kernel,
        grid_spec=grid_spec,
        out_shape=jax.ShapeDtypeStruct((parts, nvar, owned, levels), F32),
        compiler_params=pltpu.CompilerParams(vmem_limit_bytes=LIMIT),
    )(core, w_own, w_other, gx, gz, v, own, other, *sources)


SLOTS = (
    [(0, 0, c, 0) for c in (0, 1)]
    + [(0, 1, c, 0) for c in (0, 1)]
    + [(3, 0, c, 0) for c in (0, 1)]
    + [(1, 0, c, 0) for c in (0, 1)]
    + [(2, 0, 0, 1), (2, 0, 1, 1), (2, 1, 0, 1), (2, 1, 1, 1)]
    + [(3, 1, c, 0) for c in (0, 1)]
    + [(1, 1, c, 0) for c in (0, 1)]
)


def gather(keep, handed):
    half = keep.shape[0] // 2
    odd = (lax.axis_index("x") % 2).reshape(1).astype(jnp.int32)
    unit, first, second, chosen = assemble(odd, keep, handed)
    near_a = send(first, Z_NEAR)
    near_b = send(second, Z_NEAR)
    far_a = send(chosen, Y_FAR)
    up = send(unit, Y_UP)
    down = send(unit, Y_DOWN)
    far_b = send(far_a, X_PAIR)
    near_far_a = send(far_a, Z_NEAR)
    up_a = send(near_a, Y_UP)
    down_a = send(near_a, Y_DOWN)
    near_far_b = send(far_b, Z_NEAR)
    up_b = send(near_b, Y_UP)
    down_b = send(near_b, Y_DOWN)
    return (
        ((unit, 0, 0),),
        ((near_a, 2, 0), (near_b, 2, half), (far_a, 8, 0), (far_b, 9, 0)),
        ((up, 4, 0), (down, 6, 0)),
        ((near_far_a, 10, 0), (near_far_b, 11, 0)),
        ((up_a, 12, 0), (down_a, 14, 0)),
        ((up_b, 12, half), (down_b, 14, half)),
    )


def slot_table():
    zhi, y, c = lax.axis_index("zhi"), lax.axis_index("y"), lax.axis_index("core")
    odd = lax.axis_index("x") & 1
    slot = jnp.arange(len(SLOTS), dtype=jnp.int32)
    picks = (sum(jnp.where(slot == i, d[n], 0) for i, d in enumerate(SLOTS)) for n in range(4))
    dy, dz, dc, dx = picks
    return ((zhi ^ dz) * 8 + ((y + dy) & 3) * 2 + (c ^ dc ^ (dx & odd))).astype(jnp.int32)


def shards(control, perturb, member_weights, blocks, block_cols, vertical):
    nodes_all, mem_dev, lev_dev = control.shape
    members_all = mem_dev * 16
    groups, owned = 8, nodes_all // 128
    core_index = lax.axis_index("core")
    core = core_index.reshape(1).astype(jnp.int32)
    other = 1 - core
    stored = blocks[:, 0]
    handed = send(pack(other, stored), CORE)
    stages = gather(pack(core, stored), handed)
    x = control.transpose(1, 2, 0).reshape(mem_dev * lev_dev, nodes_all)
    x_other = send(x, CORE)
    xc = prep_call(core, x, x_other)
    weights = member_weights / math.sqrt(members_all - 1)
    weights_other = send(weights, CORE)
    fields = perturb.transpose(0, 2, 1, 3)
    fields_other = send(fields, CORE)
    shape = (groups, 2, owned) + fields.shape[1:]
    fields, fields_other = fields.reshape(shape), fields_other.reshape(shape)
    table = slot_table()
    shape = (2, nodes_all // 2, nodes_all // 2)
    gx = lax.axis_index("x").reshape(1).astype(jnp.int32)
    gz = lax.axis_index("zlo").reshape(1).astype(jnp.int32)
    dense, halves = None, ()
    for stage, parts in enumerate(stages):
        pieces, plan = [p[0] for p in parts], tuple(p[1:] for p in parts)
        args = (block_cols, core, table, gx, gz, pieces, plan, shape)
        dense = place_call(*args, dense, halves)
        if stage >= len(stages) - 2:
            halves += (forward_call(xc, dense, len(halves) * shape[2] // 2),)
    parts = (REACH[:CUT], REACH[CUT:])
    sums, last = [], ()
    for part in parts:
        give = backward_call(other, gx, gz, part, *halves, dense, after=last)
        last = (give,)
        sums.append(send(give, CORE))
    ready = []
    for part, added in zip(parts, sums):
        ready += backward_call(core, gx, gz, part, *halves, dense, (added,), tuple(ready[:1]))
    sources = []
    for value, pairs in zip(ready, LEVELS[:-1]):
        sources.append(send(value, pairs))
    sources.append(ready[-1])
    out = post_call(
        core, weights, weights_other, gx, gz, vertical, fields, fields_other, sources
    )
    out = lax.all_to_all(out, ("zhi", "y"), split_axis=0, concat_axis=0, tiled=True)
    return jnp.sum(out, axis=0).transpose(1, 0, 2)


def solution(mesh):
    fine = Mesh(mesh.devices.reshape(4, 2, 2, 4, 2), AXES)
    lev, mem = ("x", "zlo"), ("zhi", "y", "core")
    in_specs = (
        P(None, mem, lev),
        P(lev, mem, None, None),
        P(mem),
        P(None, mem, None, None),
        P(),
        P(),
    )
    out_specs = P(AXES, None, None)

    return jax.shard_map(shards, mesh=fine, in_specs=in_specs, out_specs=out_specs, check_vma=False)
```

```python
import functools
import math

import jax
import jax.numpy as jnp
from jax import lax
from jax.experimental import pallas as pl
from jax.experimental.pallas import tpu as pltpu
from jax.sharding import Mesh
from jax.sharding import PartitionSpec as P

BF = jnp.bfloat16
F32 = jnp.float32
AXES = ("x", "zlo", "zhi", "y", "core")


def coords(d):
    x, zlo, zhi, y, c = d // 32, d // 16 % 2, d // 8 % 2, d // 2 % 4, d % 2
    return x, y, 2 * zhi + zlo, c


def device(x, y, z, c):
    return (x % 4) * 32 + (z % 2) * 16 + (z // 2) * 8 + (y % 4) * 2 + c


def perm(move):
    return [(d, device(*move(*coords(d)))) for d in range(128)]


Z_NEAR = perm(lambda x, y, z, c: (x, y, 3 - z, c))
Y_UP = perm(lambda x, y, z, c: (x, y + 1, z, c))
Y_DOWN = perm(lambda x, y, z, c: (x, y - 1, z, c))
Y_FAR = perm(lambda x, y, z, c: (x, y + 2, z, c))
X_PAIR = perm(lambda x, y, z, c: (x ^ 1, y, z, c))
REACH = ((1, 1), (3, 0), (2, 1), (1, 0), (3, 1), (2, 0), (0, 1), (0, 0))
LEVELS = tuple(
    perm(lambda x, y, z, c, dx=dx, dz=dz: (x + dx, y, z ^ dz, c)) for dx, dz in REACH
)
CUT = 4
CORE = perm(lambda x, y, z, c: (x, y, z, 1 - c))
LIMIT = 20 * 1024 * 1024
VMEM = pl.BlockSpec(memory_space=pltpu.VMEM)
SMEM = pl.BlockSpec(memory_space=pltpu.SMEM)


def send(value, pairs):
    return lax.ppermute(value, AXES, pairs)


def split2(x):
    hi = x.astype(BF)
    return hi, (x - hi.astype(F32)).astype(BF)


def pack_kernel(core_ref, b_ref, give_ref, keep_ref):
    rows = keep_ref.shape[0]
    for out, half in ((give_ref, 1 - core_ref[0]), (keep_ref, core_ref[0])):
        for t in range(rows):
            i = 2 * (half * rows + t)
            two = jnp.concatenate([b_ref[i], b_ref[i + 1]], axis=0).astype(F32)
            out[t] = two.T.astype(BF)


def pack(core, b):
    n, p, q = b.shape
    shape = jax.ShapeDtypeStruct((n // 4, q, 2 * p), BF)
    return pl.pallas_call(
        pack_kernel,
        out_shape=(shape, shape),
        in_specs=[SMEM, VMEM],
        out_specs=(VMEM, VMEM),
        compiler_params=pltpu.CompilerParams(vmem_limit_bytes=LIMIT),
    )(core, b)


def assemble_kernel(odd_ref, keep_ref, handed_ref, unit_ref, first_ref, second_ref, far_ref):
    half = first_ref.shape[1]
    for slot, ref in enumerate((keep_ref, handed_ref)):
        unit_ref[slot] = ref[...]
        first_ref[slot] = ref[:half]
        second_ref[slot] = ref[half:]

        @pl.when(odd_ref[0] == slot)
        def _(ref=ref):
            far_ref[0] = ref[...]


def assemble(odd, keep, handed):
    rows, q, p = keep.shape
    counts = ((2, rows), (2, rows // 2), (2, rows // 2), (1, rows))
    return pl.pallas_call(
        assemble_kernel,
        out_shape=tuple(jax.ShapeDtypeStruct(c + (q, p), BF) for c in counts),
        in_specs=[SMEM, VMEM, VMEM],
        out_specs=(VMEM,) * 4,
        compiler_params=pltpu.CompilerParams(vmem_limit_bytes=LIMIT),
    )(odd, keep, handed)


def prep_kernel(core_ref, own_ref, other_ref, o_ref):
    core = core_ref[0]
    columns, width = own_ref.shape
    for ref, c in ((own_ref, core), (other_ref, 1 - core)):
        value = ref[...]
        for owner in range(2):
            begin = [64 * b + 32 * owner for b in range(width // 64)]
            runs = jnp.concatenate([value[:, b : b + 32] for b in begin], axis=1)
            hi, lo = split2(runs)
            o_ref[owner, pl.ds(pl.multiple_of(c * columns, columns), columns)] = hi
            o_ref[owner, pl.ds(pl.multiple_of((2 + c) * columns, columns), columns)] = lo


def prep_call(core, own, other):
    columns, n_all = own.shape
    width = 1024
    return pl.pallas_call(
        prep_kernel,
        grid=(n_all // width,),
        out_shape=jax.ShapeDtypeStruct((2, 4 * columns, n_all // 2), BF),
        in_specs=[SMEM] + [pl.BlockSpec((columns, width), lambda g: (0, g))] * 2,
        out_specs=pl.BlockSpec((2, 4 * columns, width // 2), lambda g: (0, 0, g)),
        compiler_params=pltpu.CompilerParams(vmem_limit_bytes=LIMIT),
    )(core, own, other)


def place_kernel(plan, zero_first, cols_ref, core_ref, jtab_ref, gx_ref, gz_ref, *rest):
    pieces, bt = rest[: len(plan)], rest[-1]
    n_half, lanes = bt.shape[1:]
    first = core_ref[0] * (cols_ref.shape[1] // 2)
    if zero_first:

        def zero(r, _):
            s = pl.ds(pl.multiple_of(r * 64, 64), 64)
            bt[0, s] = jnp.zeros((64, lanes), BF)
            bt[1, s] = jnp.zeros((64, lanes), BF)
            return 0

        lax.fori_loop(0, n_half // 64, zero, 0)
    for piece, (slot, start) in zip(pieces, plan):
        for s in range(piece.shape[0]):
            j = jtab_ref[slot + s]
            for t in range(piece.shape[1]):
                tile = piece[s, t]
                for h in range(2):
                    i = 2 * (start + t) + h
                    row = pl.multiple_of(cols_ref[j, first + i] * 32, 32)
                    for owner in range(2):
                        part = tile[owner * 32 : owner * 32 + 32, h * 64 : h * 64 + 64]
                        bt[owner, pl.ds(row, 32), i * 64 : i * 64 + 64] = part


def place_call(cols, core, jtab, gx, gz, pieces, plan, shape, dense=None, after=()):
    given = () if dense is None else (dense,)
    position = 5 + len(pieces) + len(after)
    return pl.pallas_call(
        functools.partial(place_kernel, plan, dense is None),
        out_shape=jax.ShapeDtypeStruct(shape, BF),
        in_specs=[SMEM] * 5
        + [VMEM] * len(pieces)
        + [pl.BlockSpec(memory_space=pl.ANY)] * len(after)
        + [VMEM] * len(given),
        out_specs=VMEM,
        input_output_aliases={position: 0} if given else {},
        compiler_params=pltpu.CompilerParams(vmem_limit_bytes=LIMIT),
    )(cols, core, jtab, gx, gz, *pieces, *after, *given)


def forward_kernel(begin, x_ref, bt, f_ref):
    columns = x_ref.shape[1] // 2
    s = slice(begin, begin + f_ref.shape[1])
    f = jnp.dot(x_ref[0], bt[0, :, s], preferred_element_type=F32)
    f += jnp.dot(x_ref[1], bt[1, :, s], preferred_element_type=F32)
    hi, lo = split2(f[:columns] + f[columns:])
    f_ref[0:columns] = hi
    f_ref[columns:] = lo


def backward_kernel(reach, adds, skips, owner_ref, gx_ref, gz_ref, fa_ref, fb_ref, bt, *rest):
    columns = fa_ref.shape[0] // 2
    outs = rest[adds + skips :]
    width = outs[0].shape[-1]
    cut = fa_ref.shape[1]
    dims = (((1,), (1,)), ((), ()))
    for g, (dx, dz) in enumerate(reach):
        group = ((gx_ref[0] + dx) & 3) * 2 + (gz_ref[0] ^ dz)
        s = pl.ds(pl.multiple_of(group * width, width), width)
        rows = bt.at[owner_ref[0], s]
        y = lax.dot_general(fa_ref[...], rows[:, :cut], dims, preferred_element_type=F32)
        y += lax.dot_general(fb_ref[...], rows[:, cut:], dims, preferred_element_type=F32)
        y = y[:columns] + y[columns:]
        if adds:
            outs[g][...] = y + rest[0][g]
        else:
            outs[0][g] = y


def forward_call(x, dense, begin):
    lanes = dense.shape[2] // 2
    flops = 4 * x.shape[1] * x.shape[2] * lanes
    return pl.pallas_call(
        functools.partial(forward_kernel, begin),
        out_shape=jax.ShapeDtypeStruct((x.shape[1], lanes), BF),
        in_specs=[VMEM, VMEM],
        out_specs=VMEM,
        compiler_params=pltpu.CompilerParams(vmem_limit_bytes=LIMIT),
        cost_estimate=pl.CostEstimate(flops=flops, bytes_accessed=8 << 20, transcendentals=0),
    )(x, dense)


def backward_call(owner, gx, gz, reach, fa, fb, dense, added=(), after=()):
    n_half, lanes = dense.shape[1:]
    count = len(reach)
    one = (fa.shape[0] // 2, n_half // 8)
    flops = 2 * fa.shape[0] * n_half * lanes * count // 8
    if added:
        out_shape = (jax.ShapeDtypeStruct(one, F32),) * count
    else:
        out_shape = jax.ShapeDtypeStruct((count,) + one, F32)
    return pl.pallas_call(
        functools.partial(backward_kernel, reach, len(added), len(after)),
        out_shape=out_shape,
        in_specs=[SMEM] * 3
        + [VMEM] * (3 + len(added))
        + [pl.BlockSpec(memory_space=pl.ANY)] * len(after),
        out_specs=(VMEM,) * count if added else VMEM,
        compiler_params=pltpu.CompilerParams(vmem_limit_bytes=LIMIT),
        cost_estimate=pl.CostEstimate(flops=flops, bytes_accessed=4 << 20, transcendentals=0),
    )(owner, gx, gz, fa, fb, dense, *added, *after)


def post_kernel(core_ref, w_own_ref, w_other_ref, gx_ref, gz_ref, v_ref, own_ref, other_ref, *rest):
    sources, (o_ref, loc, vt) = rest[:-3], rest[-3:]
    core = core_ref[0]
    groups = len(sources)
    block = loc.shape[1]
    nodes = pl.ds(pl.multiple_of(pl.program_id(0) * block, block), block)
    members = w_own_ref.shape[0]
    inner = v_ref.shape[1] // groups
    vt[...] = v_ref[...].T
    came = [((gx_ref[0] - dx) & 3) * 2 + (gz_ref[0] ^ dz) for dx, dz in REACH]
    begin = [pl.multiple_of(lev * inner, inner) for lev in came]
    vhi, vlo = split2(jnp.concatenate([vt[pl.ds(b, inner)] for b in begin], axis=0))
    for m in range(2 * members):
        rows = slice(m * inner, (m + 1) * inner)
        column = jnp.concatenate([source[rows, nodes] for source in sources], axis=0)
        hi, lo = split2(column.T)
        part = jnp.dot(hi, vhi, preferred_element_type=F32)
        part += jnp.dot(lo, vhi, preferred_element_type=F32)
        part += jnp.dot(hi, vlo, preferred_element_type=F32)
        c, k = divmod(m, members)
        loc[c, :, k, :] = part * jnp.where(core == c, w_own_ref[k], w_other_ref[k])
    _, nvar, owned, _ = o_ref.shape
    for d in range(o_ref.shape[0]):
        rows = pl.ds(d * owned, owned)
        near = loc[core, rows]
        far = loc[1 - core, rows]
        for v in range(nvar):
            both = own_ref[d, 0, :, v].astype(F32) * near
            both += other_ref[d, 0, :, v].astype(F32) * far
            o_ref[d, v] = jnp.sum(both, axis=1)


def post_call(core, w_own, w_other, gx, gz, v, own, other, sources):
    parts, _, owned, nvar, members, levels = own.shape
    nodes = sources[0].shape[1]
    block = 128
    step = block // owned
    field = pl.BlockSpec(
        (step, 1, owned, nvar, members, levels), lambda g, c: (g, c[0], 0, 0, 0, 0)
    )
    grid_spec = pltpu.PrefetchScalarGridSpec(
        num_scalar_prefetch=1,
        grid=(nodes // block,),
        in_specs=[SMEM] * 4
        + [pl.BlockSpec((levels, levels), lambda g, c: (0, 0)), field, field]
        + [VMEM] * len(sources),
        out_specs=pl.BlockSpec((step, nvar, owned, levels), lambda g, c: (g, 0, 0, 0)),
        scratch_shapes=[
            pltpu.VMEM((2, block, members, levels), F32),
            pltpu.VMEM((levels, levels), F32),
        ],
    )
    return pl.pallas_call(
        post_kernel,
        grid_spec=grid_spec,
        out_shape=jax.ShapeDtypeStruct((parts, nvar, owned, levels), F32),
        compiler_params=pltpu.CompilerParams(vmem_limit_bytes=LIMIT),
    )(core, w_own, w_other, gx, gz, v, own, other, *sources)


SLOTS = (
    [(0, 0, c, 0) for c in (0, 1)]
    + [(0, 1, c, 0) for c in (0, 1)]
    + [(3, 0, c, 0) for c in (0, 1)]
    + [(1, 0, c, 0) for c in (0, 1)]
    + [(2, 0, 0, 1), (2, 0, 1, 1), (2, 1, 0, 1), (2, 1, 1, 1)]
    + [(3, 1, c, 0) for c in (0, 1)]
    + [(1, 1, c, 0) for c in (0, 1)]
)


def gather(keep, handed):
    half = keep.shape[0] // 2
    odd = (lax.axis_index("x") % 2).reshape(1).astype(jnp.int32)
    unit, first, second, chosen = assemble(odd, keep, handed)
    near_a = send(first, Z_NEAR)
    near_b = send(second, Z_NEAR)
    far_a = send(chosen, Y_FAR)
    up = send(unit, Y_UP)
    down = send(unit, Y_DOWN)
    far_b = send(far_a, X_PAIR)
    near_far_a = send(far_a, Z_NEAR)
    up_a = send(near_a, Y_UP)
    down_a = send(near_a, Y_DOWN)
    near_far_b = send(far_b, Z_NEAR)
    up_b = send(near_b, Y_UP)
    down_b = send(near_b, Y_DOWN)
    return (
        ((unit, 0, 0),),
        ((near_a, 2, 0), (near_b, 2, half), (far_a, 8, 0), (far_b, 9, 0))
        + ((up, 4, 0), (down, 6, 0), (near_far_a, 10, 0), (near_far_b, 11, 0)),
        ((up_a, 12, 0), (down_a, 14, 0)),
        ((up_b, 12, half), (down_b, 14, half)),
    )


def slot_table():
    zhi, y, c = lax.axis_index("zhi"), lax.axis_index("y"), lax.axis_index("core")
    odd = lax.axis_index("x") & 1
    slot = jnp.arange(len(SLOTS), dtype=jnp.int32)
    picks = (sum(jnp.where(slot == i, d[n], 0) for i, d in enumerate(SLOTS)) for n in range(4))
    dy, dz, dc, dx = picks
    return ((zhi ^ dz) * 8 + ((y + dy) & 3) * 2 + (c ^ dc ^ (dx & odd))).astype(jnp.int32)


def shards(control, perturb, member_weights, blocks, block_cols, vertical):
    nodes_all, mem_dev, lev_dev = control.shape
    members_all = mem_dev * 16
    groups, owned = 8, nodes_all // 128
    core_index = lax.axis_index("core")
    core = core_index.reshape(1).astype(jnp.int32)
    other = 1 - core
    stored = blocks[:, 0]
    give, own = pack(core, stored)
    stages = gather(own, send(give, CORE))
    x = control.transpose(1, 2, 0).reshape(mem_dev * lev_dev, nodes_all)
    x_other = send(x, CORE)
    xc = prep_call(core, x, x_other)
    weights = member_weights / math.sqrt(members_all - 1)
    weights_other = send(weights, CORE)
    fields = perturb.transpose(0, 2, 1, 3)
    fields_other = send(fields, CORE)
    shape = (groups, 2, owned) + fields.shape[1:]
    fields, fields_other = fields.reshape(shape), fields_other.reshape(shape)
    table = slot_table()
    shape = (2, nodes_all // 2, nodes_all // 2)
    gx = lax.axis_index("x").reshape(1).astype(jnp.int32)
    gz = lax.axis_index("zlo").reshape(1).astype(jnp.int32)
    dense, halves = None, ()
    for stage, parts in enumerate(stages):
        pieces, plan = [p[0] for p in parts], tuple(p[1:] for p in parts)
        args = (block_cols.T, core, table, gx, gz, pieces, plan, shape)
        dense = place_call(*args, dense, halves)
        if stage >= len(stages) - 2:
            halves += (forward_call(xc, dense, len(halves) * shape[2] // 2),)
    parts = (REACH[:CUT], REACH[CUT:])
    sums, last = [], ()
    for part in parts:
        give = backward_call(other, gx, gz, part, *halves, dense, after=last)
        last = (give,)
        sums.append(send(give, CORE))
    ready = []
    for part, added in zip(parts, sums):
        ready += backward_call(core, gx, gz, part, *halves, dense, (added,), tuple(ready[:1]))
    sources = []
    for value, pairs in zip(ready, LEVELS[:-1]):
        sources.append(send(value, pairs))
    sources.append(ready[-1])
    out = post_call(
        core, weights, weights_other, gx, gz, vertical, fields, fields_other, sources
    )
    out = lax.all_to_all(out, ("zhi", "y"), split_axis=0, concat_axis=0, tiled=True)
    return jnp.sum(out, axis=0).transpose(1, 0, 2)


def solution(mesh):
    fine = Mesh(mesh.devices.reshape(4, 2, 2, 4, 2), AXES)
    lev, mem = ("x", "zlo"), ("zhi", "y", "core")
    in_specs = (
        P(None, mem, lev),
        P(lev, mem, None, None),
        P(mem),
        P(None, mem, None, None),
        P(),
        P(),
    )
    out_specs = P(AXES, None, None)

    return jax.shard_map(shards, mesh=fine, in_specs=in_specs, out_specs=out_specs, check_vma=False)
```

```python
import functools
import math

import jax
import jax.numpy as jnp
from jax import lax
from jax.experimental import pallas as pl
from jax.experimental.pallas import tpu as pltpu
from jax.sharding import Mesh
from jax.sharding import PartitionSpec as P

BF = jnp.bfloat16
F32 = jnp.float32
AXES = ("x", "zlo", "zhi", "y", "core")


def coords(d):
    x, zlo, zhi, y, c = d // 32, d // 16 % 2, d // 8 % 2, d // 2 % 4, d % 2
    return x, y, 2 * zhi + zlo, c


def device(x, y, z, c):
    return (x % 4) * 32 + (z % 2) * 16 + (z // 2) * 8 + (y % 4) * 2 + c


def perm(move):
    return [(d, device(*move(*coords(d)))) for d in range(128)]


Z_NEAR = perm(lambda x, y, z, c: (x, y, 3 - z, c))
Y_UP = perm(lambda x, y, z, c: (x, y + 1, z, c))
Y_DOWN = perm(lambda x, y, z, c: (x, y - 1, z, c))
Y_FAR = perm(lambda x, y, z, c: (x, y + 2, z, c))
X_PAIR = perm(lambda x, y, z, c: (x ^ 1, y, z, c))
REACH = ((1, 1), (3, 0), (2, 1), (1, 0), (3, 1), (2, 0), (0, 1), (0, 0))
LEVELS = tuple(
    perm(lambda x, y, z, c, dx=dx, dz=dz: (x + dx, y, z ^ dz, c)) for dx, dz in REACH
)
CUTS = (0, 2, 5, 8)
CORE = perm(lambda x, y, z, c: (x, y, z, 1 - c))
LIMIT = 20 * 1024 * 1024
VMEM = pl.BlockSpec(memory_space=pltpu.VMEM)
SMEM = pl.BlockSpec(memory_space=pltpu.SMEM)


def send(value, pairs):
    return lax.ppermute(value, AXES, pairs)


def split2(x):
    hi = x.astype(BF)
    return hi, (x - hi.astype(F32)).astype(BF)


def pack_kernel(core_ref, b_ref, give_ref, keep_ref):
    rows = keep_ref.shape[0]
    for out, half in ((give_ref, 1 - core_ref[0]), (keep_ref, core_ref[0])):
        for t in range(rows):
            i = 2 * (half * rows + t)
            two = jnp.concatenate([b_ref[i], b_ref[i + 1]], axis=0).astype(F32)
            out[t] = two.T.astype(BF)


def pack(core, b):
    n, p, q = b.shape
    shape = jax.ShapeDtypeStruct((n // 4, q, 2 * p), BF)
    return pl.pallas_call(
        pack_kernel,
        out_shape=(shape, shape),
        in_specs=[SMEM, VMEM],
        out_specs=(VMEM, VMEM),
        compiler_params=pltpu.CompilerParams(vmem_limit_bytes=LIMIT),
    )(core, b)


def assemble_kernel(odd_ref, keep_ref, handed_ref, unit_ref, first_ref, second_ref, far_ref):
    half = first_ref.shape[1]
    for slot, ref in enumerate((keep_ref, handed_ref)):
        unit_ref[slot] = ref[...]
        first_ref[slot] = ref[:half]
        second_ref[slot] = ref[half:]

        @pl.when(odd_ref[0] == slot)
        def _(ref=ref):
            far_ref[0] = ref[...]


def assemble(odd, keep, handed):
    rows, q, p = keep.shape
    counts = ((2, rows), (2, rows // 2), (2, rows // 2), (1, rows))
    return pl.pallas_call(
        assemble_kernel,
        out_shape=tuple(jax.ShapeDtypeStruct(c + (q, p), BF) for c in counts),
        in_specs=[SMEM, VMEM, VMEM],
        out_specs=(VMEM,) * 4,
        compiler_params=pltpu.CompilerParams(vmem_limit_bytes=LIMIT),
    )(odd, keep, handed)


def prep_kernel(core_ref, own_ref, other_ref, o_ref):
    core = core_ref[0]
    columns, width = own_ref.shape
    for ref, c in ((own_ref, core), (other_ref, 1 - core)):
        value = ref[...]
        for owner in range(2):
            begin = [64 * b + 32 * owner for b in range(width // 64)]
            runs = jnp.concatenate([value[:, b : b + 32] for b in begin], axis=1)
            hi, lo = split2(runs)
            o_ref[owner, pl.ds(pl.multiple_of(c * columns, columns), columns)] = hi
            o_ref[owner, pl.ds(pl.multiple_of((2 + c) * columns, columns), columns)] = lo


def prep_call(core, own, other):
    columns, n_all = own.shape
    width = 1024
    return pl.pallas_call(
        prep_kernel,
        grid=(n_all // width,),
        out_shape=jax.ShapeDtypeStruct((2, 4 * columns, n_all // 2), BF),
        in_specs=[SMEM] + [pl.BlockSpec((columns, width), lambda g: (0, g))] * 2,
        out_specs=pl.BlockSpec((2, 4 * columns, width // 2), lambda g: (0, 0, g)),
        compiler_params=pltpu.CompilerParams(vmem_limit_bytes=LIMIT),
    )(core, own, other)


def place_kernel(plan, zero_first, cols_ref, core_ref, jtab_ref, gx_ref, gz_ref, *rest):
    pieces, bt = rest[: len(plan)], rest[-1]
    n_half, lanes = bt.shape[1:]
    first = core_ref[0] * (cols_ref.shape[1] // 2)
    if zero_first:

        def zero(r, _):
            s = pl.ds(pl.multiple_of(r * 64, 64), 64)
            bt[0, s] = jnp.zeros((64, lanes), BF)
            bt[1, s] = jnp.zeros((64, lanes), BF)
            return 0

        lax.fori_loop(0, n_half // 64, zero, 0)
    for piece, (slot, start) in zip(pieces, plan):
        for s in range(piece.shape[0]):
            j = jtab_ref[slot + s]
            for t in range(piece.shape[1]):
                tile = piece[s, t]
                for h in range(2):
                    i = 2 * (start + t) + h
                    row = pl.multiple_of(cols_ref[j, first + i] * 32, 32)
                    for owner in range(2):
                        part = tile[owner * 32 : owner * 32 + 32, h * 64 : h * 64 + 64]
                        bt[owner, pl.ds(row, 32), i * 64 : i * 64 + 64] = part


def place_call(cols, core, jtab, gx, gz, pieces, plan, shape, dense=None, after=()):
    given = () if dense is None else (dense,)
    position = 5 + len(pieces) + len(after)
    return pl.pallas_call(
        functools.partial(place_kernel, plan, dense is None),
        out_shape=jax.ShapeDtypeStruct(shape, BF),
        in_specs=[SMEM] * 5
        + [VMEM] * len(pieces)
        + [pl.BlockSpec(memory_space=pl.ANY)] * len(after)
        + [VMEM] * len(given),
        out_specs=VMEM,
        input_output_aliases={position: 0} if given else {},
        compiler_params=pltpu.CompilerParams(vmem_limit_bytes=LIMIT),
    )(cols, core, jtab, gx, gz, *pieces, *after, *given)


def forward_kernel(begin, x_ref, bt, f_ref):
    columns = x_ref.shape[1] // 2
    s = slice(begin, begin + f_ref.shape[1])
    f = jnp.dot(x_ref[0], bt[0, :, s], preferred_element_type=F32)
    f += jnp.dot(x_ref[1], bt[1, :, s], preferred_element_type=F32)
    hi, lo = split2(f[:columns] + f[columns:])
    f_ref[0:columns] = hi
    f_ref[columns:] = lo


def backward_kernel(reach, adds, skips, owner_ref, gx_ref, gz_ref, fa_ref, fb_ref, bt, *rest):
    columns = fa_ref.shape[0] // 2
    outs = rest[adds + skips :]
    width = outs[0].shape[-1]
    cut = fa_ref.shape[1]
    dims = (((1,), (1,)), ((), ()))
    for g, (dx, dz) in enumerate(reach):
        group = ((gx_ref[0] + dx) & 3) * 2 + (gz_ref[0] ^ dz)
        s = pl.ds(pl.multiple_of(group * width, width), width)
        rows = bt.at[owner_ref[0], s]
        y = lax.dot_general(fa_ref[...], rows[:, :cut], dims, preferred_element_type=F32)
        y += lax.dot_general(fb_ref[...], rows[:, cut:], dims, preferred_element_type=F32)
        y = y[:columns] + y[columns:]
        if adds:
            outs[g][...] = y + rest[0][g]
        else:
            outs[0][g] = y


def forward_call(x, dense, begin):
    lanes = dense.shape[2] // 2
    flops = 4 * x.shape[1] * x.shape[2] * lanes
    return pl.pallas_call(
        functools.partial(forward_kernel, begin),
        out_shape=jax.ShapeDtypeStruct((x.shape[1], lanes), BF),
        in_specs=[VMEM, VMEM],
        out_specs=VMEM,
        compiler_params=pltpu.CompilerParams(vmem_limit_bytes=LIMIT),
        cost_estimate=pl.CostEstimate(flops=flops, bytes_accessed=8 << 20, transcendentals=0),
    )(x, dense)


def backward_call(owner, gx, gz, reach, fa, fb, dense, added=(), after=()):
    n_half, lanes = dense.shape[1:]
    count = len(reach)
    one = (fa.shape[0] // 2, n_half // 8)
    flops = 2 * fa.shape[0] * n_half * lanes * count // 8
    if added:
        out_shape = (jax.ShapeDtypeStruct(one, F32),) * count
    else:
        out_shape = jax.ShapeDtypeStruct((count,) + one, F32)
    return pl.pallas_call(
        functools.partial(backward_kernel, reach, len(added), len(after)),
        out_shape=out_shape,
        in_specs=[SMEM] * 3
        + [VMEM] * (3 + len(added))
        + [pl.BlockSpec(memory_space=pl.ANY)] * len(after),
        out_specs=(VMEM,) * count if added else VMEM,
        compiler_params=pltpu.CompilerParams(vmem_limit_bytes=LIMIT),
        cost_estimate=pl.CostEstimate(flops=flops, bytes_accessed=4 << 20, transcendentals=0),
    )(owner, gx, gz, fa, fb, dense, *added, *after)


def localize(core, w_own_ref, w_other_ref, gx_ref, gz_ref, v_ref, reach, sources, loc, vt):
    groups = 8
    block = loc.shape[1]
    nodes = pl.ds(pl.multiple_of(pl.program_id(0) * block, block), block)
    members = w_own_ref.shape[0]
    inner = v_ref.shape[1] // groups
    vt[...] = v_ref[...].T
    came = [((gx_ref[0] - dx) & 3) * 2 + (gz_ref[0] ^ dz) for dx, dz in reach]
    begin = [pl.multiple_of(lev * inner, inner) for lev in came]
    vhi, vlo = split2(jnp.concatenate([vt[pl.ds(b, inner)] for b in begin], axis=0))
    for m in range(2 * members):
        rows = slice(m * inner, (m + 1) * inner)
        column = jnp.concatenate([source[rows, nodes] for source in sources], axis=0)
        hi, lo = split2(column.T)
        part = jnp.dot(hi, vhi, preferred_element_type=F32)
        part += jnp.dot(lo, vhi, preferred_element_type=F32)
        part += jnp.dot(hi, vlo, preferred_element_type=F32)
        c, k = divmod(m, members)
        loc[c, :, k, :] = part * jnp.where(core == c, w_own_ref[k], w_other_ref[k])


def early_kernel(reach, core_ref, w_own_ref, w_other_ref, gx_ref, gz_ref, v_ref, *rest):
    sources, (loc, vt) = rest[:-2], rest[-2:]
    localize(
        core_ref[0], w_own_ref, w_other_ref, gx_ref, gz_ref, v_ref, reach, sources, loc, vt
    )


def early_call(core, w_own, w_other, gx, gz, v, reach, sources):
    levels, members = v.shape[0], w_own.shape[0]
    nodes = sources[0].shape[1]
    block = 128
    return pl.pallas_call(
        functools.partial(early_kernel, reach),
        grid=(nodes // block,),
        out_shape=jax.ShapeDtypeStruct((2, nodes, members, levels), F32),
        in_specs=[SMEM] * 5
        + [pl.BlockSpec((levels, levels), lambda g: (0, 0))]
        + [VMEM] * len(sources),
        out_specs=pl.BlockSpec((2, block, members, levels), lambda g: (0, g, 0, 0)),
        scratch_shapes=[pltpu.VMEM((levels, levels), F32)],
        compiler_params=pltpu.CompilerParams(vmem_limit_bytes=LIMIT),
    )(core, w_own, w_other, gx, gz, v, *sources)


def post_kernel(reach, core_ref, w_own_ref, w_other_ref, gx_ref, gz_ref, v_ref, *rest):
    own_ref, other_ref, early_ref = rest[:3]
    sources, (o_ref, loc, vt) = rest[3:-3], rest[-3:]
    core = core_ref[0]
    localize(core, w_own_ref, w_other_ref, gx_ref, gz_ref, v_ref, reach, sources, loc, vt)
    _, nvar, owned, _ = o_ref.shape
    for d in range(o_ref.shape[0]):
        rows = pl.ds(d * owned, owned)
        near = loc[core, rows] + early_ref[core, rows]
        far = loc[1 - core, rows] + early_ref[1 - core, rows]
        for v in range(nvar):
            both = own_ref[d, 0, :, v].astype(F32) * near
            both += other_ref[d, 0, :, v].astype(F32) * far
            o_ref[d, v] = jnp.sum(both, axis=1)


def post_call(core, w_own, w_other, gx, gz, v, own, other, early, reach, sources):
    parts, _, owned, nvar, members, levels = own.shape
    nodes = sources[0].shape[1]
    block = 128
    step = block // owned
    field = pl.BlockSpec(
        (step, 1, owned, nvar, members, levels), lambda g, c: (g, c[0], 0, 0, 0, 0)
    )
    grid_spec = pltpu.PrefetchScalarGridSpec(
        num_scalar_prefetch=1,
        grid=(nodes // block,),
        in_specs=[SMEM] * 4
        + [pl.BlockSpec((levels, levels), lambda g, c: (0, 0)), field, field]
        + [pl.BlockSpec((2, block, members, levels), lambda g, c: (0, g, 0, 0))]
        + [VMEM] * len(sources),
        out_specs=pl.BlockSpec((step, nvar, owned, levels), lambda g, c: (g, 0, 0, 0)),
        scratch_shapes=[
            pltpu.VMEM((2, block, members, levels), F32),
            pltpu.VMEM((levels, levels), F32),
        ],
    )
    return pl.pallas_call(
        functools.partial(post_kernel, reach),
        grid_spec=grid_spec,
        out_shape=jax.ShapeDtypeStruct((parts, nvar, owned, levels), F32),
        compiler_params=pltpu.CompilerParams(vmem_limit_bytes=LIMIT),
    )(core, w_own, w_other, gx, gz, v, own, other, early, *sources)


SLOTS = (
    [(0, 0, c, 0) for c in (0, 1)]
    + [(0, 1, c, 0) for c in (0, 1)]
    + [(3, 0, c, 0) for c in (0, 1)]
    + [(1, 0, c, 0) for c in (0, 1)]
    + [(2, 0, 0, 1), (2, 0, 1, 1), (2, 1, 0, 1), (2, 1, 1, 1)]
    + [(3, 1, c, 0) for c in (0, 1)]
    + [(1, 1, c, 0) for c in (0, 1)]
)


def gather(keep, handed):
    half = keep.shape[0] // 2
    odd = (lax.axis_index("x") % 2).reshape(1).astype(jnp.int32)
    unit, first, second, chosen = assemble(odd, keep, handed)
    near_a = send(first, Z_NEAR)
    near_b = send(second, Z_NEAR)
    far_a = send(chosen, Y_FAR)
    up = send(unit, Y_UP)
    down = send(unit, Y_DOWN)
    far_b = send(far_a, X_PAIR)
    near_far_a = send(far_a, Z_NEAR)
    up_a = send(near_a, Y_UP)
    down_a = send(near_a, Y_DOWN)
    near_far_b = send(far_b, Z_NEAR)
    up_b = send(near_b, Y_UP)
    down_b = send(near_b, Y_DOWN)
    return (
        ((unit, 0, 0),),
        ((near_a, 2, 0), (near_b, 2, half), (far_a, 8, 0), (far_b, 9, 0))
        + ((up, 4, 0), (down, 6, 0), (near_far_a, 10, 0), (near_far_b, 11, 0)),
        ((up_a, 12, 0), (down_a, 14, 0)),
        ((up_b, 12, half), (down_b, 14, half)),
    )


def slot_table():
    zhi, y, c = lax.axis_index("zhi"), lax.axis_index("y"), lax.axis_index("core")
    odd = lax.axis_index("x") & 1
    slot = jnp.arange(len(SLOTS), dtype=jnp.int32)
    picks = (sum(jnp.where(slot == i, d[n], 0) for i, d in enumerate(SLOTS)) for n in range(4))
    dy, dz, dc, dx = picks
    return ((zhi ^ dz) * 8 + ((y + dy) & 3) * 2 + (c ^ dc ^ (dx & odd))).astype(jnp.int32)


def shards(control, perturb, member_weights, blocks, block_cols, vertical):
    nodes_all, mem_dev, lev_dev = control.shape
    members_all = mem_dev * 16
    groups, owned = 8, nodes_all // 128
    core_index = lax.axis_index("core")
    core = core_index.reshape(1).astype(jnp.int32)
    other = 1 - core
    stored = blocks[:, 0]
    give, own = pack(core, stored)
    stages = gather(own, send(give, CORE))
    x = control.transpose(1, 2, 0).reshape(mem_dev * lev_dev, nodes_all)
    x_other = send(x, CORE)
    xc = prep_call(core, x, x_other)
    weights = member_weights / math.sqrt(members_all - 1)
    weights_other = send(weights, CORE)
    fields = perturb.transpose(0, 2, 1, 3)
    fields_other = send(fields, CORE)
    shape = (groups, 2, owned) + fields.shape[1:]
    fields, fields_other = fields.reshape(shape), fields_other.reshape(shape)
    table = slot_table()
    shape = (2, nodes_all // 2, nodes_all // 2)
    gx = lax.axis_index("x").reshape(1).astype(jnp.int32)
    gz = lax.axis_index("zlo").reshape(1).astype(jnp.int32)
    dense, halves = None, ()
    for stage, parts in enumerate(stages):
        pieces, plan = [p[0] for p in parts], tuple(p[1:] for p in parts)
        args = (block_cols.T, core, table, gx, gz, pieces, plan, shape)
        dense = place_call(*args, dense, halves)
        if stage >= len(stages) - 2:
            halves += (forward_call(xc, dense, len(halves) * shape[2] // 2),)
    parts = [REACH[a:b] for a, b in zip(CUTS, CUTS[1:])]
    ready, sums, last = [], [], ()
    for n in range(len(parts) + 1):
        if n < len(parts):
            give = backward_call(other, gx, gz, parts[n], *halves, dense, after=last)
            last = (give,)
            sums.append(send(give, CORE))
        if n > 0:
            keep = backward_call(core, gx, gz, parts[n - 1], *halves, dense, (sums[n - 1],), last)
            ready += keep
            last = (keep[0],)
    sources = []
    for value, pairs in zip(ready, LEVELS[:-1]):
        sources.append(send(value, pairs))
    sources.append(ready[-1])
    late = REACH[CUTS[2] : -1]
    soon = REACH[: CUTS[2]] + REACH[-1:]
    some = sources[: CUTS[2]] + sources[-1:]
    shared = (core, weights, weights_other, gx, gz, vertical)
    early = early_call(*shared, soon, some)
    out = post_call(*shared, fields, fields_other, early, late, sources[CUTS[2] : -1])
    out = lax.all_to_all(out, ("zhi", "y"), split_axis=0, concat_axis=0, tiled=True)
    return jnp.sum(out, axis=0).transpose(1, 0, 2)


def solution(mesh):
    fine = Mesh(mesh.devices.reshape(4, 2, 2, 4, 2), AXES)
    lev, mem = ("x", "zlo"), ("zhi", "y", "core")
    in_specs = (
        P(None, mem, lev),
        P(lev, mem, None, None),
        P(mem),
        P(None, mem, None, None),
        P(),
        P(),
    )
    out_specs = P(AXES, None, None)

    return jax.shard_map(shards, mesh=fine, in_specs=in_specs, out_specs=out_specs, check_vma=False)
```

```python
import functools
import math

import jax
import jax.numpy as jnp
from jax import lax
from jax.experimental import pallas as pl
from jax.experimental.pallas import tpu as pltpu
from jax.sharding import Mesh
from jax.sharding import PartitionSpec as P

BF = jnp.bfloat16
F32 = jnp.float32
AXES = ("x", "zlo", "zhi", "y", "core")


def coords(d):
    x, zlo, zhi, y, c = d // 32, d // 16 % 2, d // 8 % 2, d // 2 % 4, d % 2
    return x, y, 2 * zhi + zlo, c


def device(x, y, z, c):
    return (x % 4) * 32 + (z % 2) * 16 + (z // 2) * 8 + (y % 4) * 2 + c


def perm(move):
    return [(d, device(*move(*coords(d)))) for d in range(128)]


Z_NEAR = perm(lambda x, y, z, c: (x, y, 3 - z, c))
Y_UP = perm(lambda x, y, z, c: (x, y + 1, z, c))
Y_DOWN = perm(lambda x, y, z, c: (x, y - 1, z, c))
Y_FAR = perm(lambda x, y, z, c: (x, y + 2, z, c))
X_PAIR = perm(lambda x, y, z, c: (x ^ 1, y, z, c))
REACH = ((1, 1), (3, 0), (2, 1), (1, 0), (3, 1), (2, 0), (0, 1), (0, 0))
LEVELS = tuple(
    perm(lambda x, y, z, c, dx=dx, dz=dz: (x + dx, y, z ^ dz, c)) for dx, dz in REACH
)
CUTS = (0, 2, 5, 8)
CORE = perm(lambda x, y, z, c: (x, y, z, 1 - c))
LIMIT = 20 * 1024 * 1024
VMEM = pl.BlockSpec(memory_space=pltpu.VMEM)
SMEM = pl.BlockSpec(memory_space=pltpu.SMEM)


def send(value, pairs):
    return lax.ppermute(value, AXES, pairs)


def split2(x):
    hi = x.astype(BF)
    return hi, (x - hi.astype(F32)).astype(BF)


def pack_kernel(core_ref, b_ref, give_ref, keep_ref):
    rows = keep_ref.shape[0]
    for out, half in ((give_ref, 1 - core_ref[0]), (keep_ref, core_ref[0])):
        for t in range(rows):
            i = 2 * (half * rows + t)
            two = jnp.concatenate([b_ref[i], b_ref[i + 1]], axis=0).astype(F32)
            out[t] = two.T.astype(BF)


def pack(core, b):
    n, p, q = b.shape
    shape = jax.ShapeDtypeStruct((n // 4, q, 2 * p), BF)
    return pl.pallas_call(
        pack_kernel,
        out_shape=(shape, shape),
        in_specs=[SMEM, VMEM],
        out_specs=(VMEM, VMEM),
        compiler_params=pltpu.CompilerParams(vmem_limit_bytes=LIMIT),
    )(core, b)


def assemble_kernel(odd_ref, keep_ref, handed_ref, unit_ref, first_ref, second_ref, far_ref):
    half = first_ref.shape[1]
    for slot, ref in enumerate((keep_ref, handed_ref)):
        unit_ref[slot] = ref[...]
        first_ref[slot] = ref[:half]
        second_ref[slot] = ref[half:]

        @pl.when(odd_ref[0] == slot)
        def _(ref=ref):
            far_ref[0] = ref[...]


def assemble(odd, keep, handed):
    rows, q, p = keep.shape
    counts = ((2, rows), (2, rows // 2), (2, rows // 2), (1, rows))
    return pl.pallas_call(
        assemble_kernel,
        out_shape=tuple(jax.ShapeDtypeStruct(c + (q, p), BF) for c in counts),
        in_specs=[SMEM, VMEM, VMEM],
        out_specs=(VMEM,) * 4,
        compiler_params=pltpu.CompilerParams(vmem_limit_bytes=LIMIT),
    )(odd, keep, handed)


def prep_kernel(core_ref, own_ref, other_ref, o_ref):
    core = core_ref[0]
    columns, width = own_ref.shape
    for ref, c in ((own_ref, core), (other_ref, 1 - core)):
        value = ref[...]
        for owner in range(2):
            begin = [64 * b + 32 * owner for b in range(width // 64)]
            runs = jnp.concatenate([value[:, b : b + 32] for b in begin], axis=1)
            hi, lo = split2(runs)
            o_ref[owner, pl.ds(pl.multiple_of(c * columns, columns), columns)] = hi
            o_ref[owner, pl.ds(pl.multiple_of((2 + c) * columns, columns), columns)] = lo


def prep_call(core, own, other):
    columns, n_all = own.shape
    width = 1024
    return pl.pallas_call(
        prep_kernel,
        grid=(n_all // width,),
        out_shape=jax.ShapeDtypeStruct((2, 4 * columns, n_all // 2), BF),
        in_specs=[SMEM] + [pl.BlockSpec((columns, width), lambda g: (0, g))] * 2,
        out_specs=pl.BlockSpec((2, 4 * columns, width // 2), lambda g: (0, 0, g)),
        compiler_params=pltpu.CompilerParams(vmem_limit_bytes=LIMIT),
    )(core, own, other)


def place_kernel(plan, zero_first, cols_ref, core_ref, jtab_ref, gx_ref, gz_ref, *rest):
    pieces, bt = rest[: len(plan)], rest[-1]
    n_half, lanes = bt.shape[1:]
    first = core_ref[0] * (cols_ref.shape[1] // 2)
    if zero_first:

        def zero(r, _):
            s = pl.ds(pl.multiple_of(r * 64, 64), 64)
            bt[0, s] = jnp.zeros((64, lanes), BF)
            bt[1, s] = jnp.zeros((64, lanes), BF)
            return 0

        lax.fori_loop(0, n_half // 64, zero, 0)
    for piece, (slot, start) in zip(pieces, plan):
        for s in range(piece.shape[0]):
            j = jtab_ref[slot + s]
            for t in range(piece.shape[1]):
                tile = piece[s, t]
                for h in range(2):
                    i = 2 * (start + t) + h
                    row = pl.multiple_of(cols_ref[j, first + i] * 32, 32)
                    for owner in range(2):
                        part = tile[owner * 32 : owner * 32 + 32, h * 64 : h * 64 + 64]
                        bt[owner, pl.ds(row, 32), i * 64 : i * 64 + 64] = part


def place_call(cols, core, jtab, gx, gz, pieces, plan, shape, dense=None, after=()):
    given = () if dense is None else (dense,)
    position = 5 + len(pieces) + len(after)
    return pl.pallas_call(
        functools.partial(place_kernel, plan, dense is None),
        out_shape=jax.ShapeDtypeStruct(shape, BF),
        in_specs=[SMEM] * 5
        + [VMEM] * len(pieces)
        + [pl.BlockSpec(memory_space=pl.ANY)] * len(after)
        + [VMEM] * len(given),
        out_specs=VMEM,
        input_output_aliases={position: 0} if given else {},
        compiler_params=pltpu.CompilerParams(vmem_limit_bytes=LIMIT),
    )(cols, core, jtab, gx, gz, *pieces, *after, *given)


def forward_kernel(begin, x_ref, bt, f_ref):
    columns = x_ref.shape[1] // 2
    s = slice(begin, begin + f_ref.shape[1])
    f = jnp.dot(x_ref[0], bt[0, :, s], preferred_element_type=F32)
    f += jnp.dot(x_ref[1], bt[1, :, s], preferred_element_type=F32)
    hi, lo = split2(f[:columns] + f[columns:])
    f_ref[0:columns] = hi
    f_ref[columns:] = lo


def backward_kernel(reach, adds, skips, owner_ref, gx_ref, gz_ref, fa_ref, fb_ref, bt, *rest):
    columns = fa_ref.shape[0] // 2
    outs = rest[adds + skips :]
    width = outs[0].shape[-1]
    cut = fa_ref.shape[1]
    dims = (((1,), (1,)), ((), ()))
    for g, (dx, dz) in enumerate(reach):
        group = ((gx_ref[0] + dx) & 3) * 2 + (gz_ref[0] ^ dz)
        s = pl.ds(pl.multiple_of(group * width, width), width)
        rows = bt.at[owner_ref[0], s]
        y = lax.dot_general(fa_ref[...], rows[:, :cut], dims, preferred_element_type=F32)
        y += lax.dot_general(fb_ref[...], rows[:, cut:], dims, preferred_element_type=F32)
        y = y[:columns] + y[columns:]
        if adds:
            outs[g][...] = y + rest[0][g]
        else:
            outs[0][g] = y


def forward_call(x, dense, begin):
    lanes = dense.shape[2] // 2
    flops = 4 * x.shape[1] * x.shape[2] * lanes
    return pl.pallas_call(
        functools.partial(forward_kernel, begin),
        out_shape=jax.ShapeDtypeStruct((x.shape[1], lanes), BF),
        in_specs=[VMEM, VMEM],
        out_specs=VMEM,
        compiler_params=pltpu.CompilerParams(vmem_limit_bytes=LIMIT),
        cost_estimate=pl.CostEstimate(flops=flops, bytes_accessed=8 << 20, transcendentals=0),
    )(x, dense)


def backward_call(owner, gx, gz, reach, fa, fb, dense, added=(), after=()):
    n_half, lanes = dense.shape[1:]
    count = len(reach)
    one = (fa.shape[0] // 2, n_half // 8)
    flops = 2 * fa.shape[0] * n_half * lanes * count // 8
    if added:
        out_shape = (jax.ShapeDtypeStruct(one, F32),) * count
    else:
        out_shape = jax.ShapeDtypeStruct((count,) + one, F32)
    return pl.pallas_call(
        functools.partial(backward_kernel, reach, len(added), len(after)),
        out_shape=out_shape,
        in_specs=[SMEM] * 3
        + [VMEM] * (3 + len(added))
        + [pl.BlockSpec(memory_space=pl.ANY)] * len(after),
        out_specs=(VMEM,) * count if added else VMEM,
        compiler_params=pltpu.CompilerParams(vmem_limit_bytes=LIMIT),
        cost_estimate=pl.CostEstimate(flops=flops, bytes_accessed=4 << 20, transcendentals=0),
    )(owner, gx, gz, fa, fb, dense, *added, *after)


def post_kernel(core_ref, w_own_ref, w_other_ref, gx_ref, gz_ref, v_ref, own_ref, other_ref, *rest):
    sources, (o_ref, loc, vt) = rest[:-3], rest[-3:]
    core = core_ref[0]
    groups = len(sources)
    block = loc.shape[1]
    nodes = pl.ds(pl.multiple_of(pl.program_id(0) * block, block), block)
    members = w_own_ref.shape[0]
    inner = v_ref.shape[1] // groups
    vt[...] = v_ref[...].T
    came = [((gx_ref[0] - dx) & 3) * 2 + (gz_ref[0] ^ dz) for dx, dz in REACH]
    begin = [pl.multiple_of(lev * inner, inner) for lev in came]
    vhi, vlo = split2(jnp.concatenate([vt[pl.ds(b, inner)] for b in begin], axis=0))
    for m in range(2 * members):
        rows = slice(m * inner, (m + 1) * inner)
        column = jnp.concatenate([source[rows, nodes] for source in sources], axis=0)
        hi, lo = split2(column.T)
        part = jnp.dot(hi, vhi, preferred_element_type=F32)
        part += jnp.dot(lo, vhi, preferred_element_type=F32)
        part += jnp.dot(hi, vlo, preferred_element_type=F32)
        c, k = divmod(m, members)
        loc[c, :, k, :] = part * jnp.where(core == c, w_own_ref[k], w_other_ref[k])
    _, nvar, owned, _ = o_ref.shape
    for d in range(o_ref.shape[0]):
        rows = pl.ds(d * owned, owned)
        near = loc[core, rows]
        far = loc[1 - core, rows]
        for v in range(nvar):
            both = own_ref[d, 0, :, v].astype(F32) * near
            both += other_ref[d, 0, :, v].astype(F32) * far
            o_ref[d, v] = jnp.sum(both, axis=1)


def post_call(core, w_own, w_other, gx, gz, v, own, other, sources):
    parts, _, owned, nvar, members, levels = own.shape
    nodes = sources[0].shape[1]
    block = 128
    step = block // owned
    field = pl.BlockSpec(
        (step, 1, owned, nvar, members, levels), lambda g, c: (g, c[0], 0, 0, 0, 0)
    )
    grid_spec = pltpu.PrefetchScalarGridSpec(
        num_scalar_prefetch=1,
        grid=(nodes // block,),
        in_specs=[SMEM] * 4
        + [pl.BlockSpec((levels, levels), lambda g, c: (0, 0)), field, field]
        + [VMEM] * len(sources),
        out_specs=pl.BlockSpec((step, nvar, owned, levels), lambda g, c: (g, 0, 0, 0)),
        scratch_shapes=[
            pltpu.VMEM((2, block, members, levels), F32),
            pltpu.VMEM((levels, levels), F32),
        ],
    )
    return pl.pallas_call(
        post_kernel,
        grid_spec=grid_spec,
        out_shape=jax.ShapeDtypeStruct((parts, nvar, owned, levels), F32),
        compiler_params=pltpu.CompilerParams(vmem_limit_bytes=LIMIT),
    )(core, w_own, w_other, gx, gz, v, own, other, *sources)


SLOTS = (
    [(0, 0, c, 0) for c in (0, 1)]
    + [(0, 1, c, 0) for c in (0, 1)]
    + [(3, 0, c, 0) for c in (0, 1)]
    + [(1, 0, c, 0) for c in (0, 1)]
    + [(2, 0, 0, 1), (2, 0, 1, 1), (2, 1, 0, 1), (2, 1, 1, 1)]
    + [(3, 1, c, 0) for c in (0, 1)]
    + [(1, 1, c, 0) for c in (0, 1)]
)


def gather(keep, handed):
    half = keep.shape[0] // 2
    odd = (lax.axis_index("x") % 2).reshape(1).astype(jnp.int32)
    unit, first, second, chosen = assemble(odd, keep, handed)
    near_a = send(first, Z_NEAR)
    near_b = send(second, Z_NEAR)
    far_a = send(chosen, Y_FAR)
    up = send(unit, Y_UP)
    down = send(unit, Y_DOWN)
    far_b = send(far_a, X_PAIR)
    near_far_a = send(far_a, Z_NEAR)
    up_a = send(near_a, Y_UP)
    down_a = send(near_a, Y_DOWN)
    near_far_b = send(far_b, Z_NEAR)
    up_b = send(near_b, Y_UP)
    down_b = send(near_b, Y_DOWN)
    return (
        ((unit, 0, 0),),
        ((near_a, 2, 0), (near_b, 2, half), (far_a, 8, 0), (far_b, 9, 0))
        + ((up, 4, 0), (down, 6, 0), (near_far_a, 10, 0), (near_far_b, 11, 0)),
        ((up_a, 12, 0), (down_a, 14, 0)),
        ((up_b, 12, half), (down_b, 14, half)),
    )


def slot_table():
    zhi, y, c = lax.axis_index("zhi"), lax.axis_index("y"), lax.axis_index("core")
    odd = lax.axis_index("x") & 1
    slot = jnp.arange(len(SLOTS), dtype=jnp.int32)
    picks = (sum(jnp.where(slot == i, d[n], 0) for i, d in enumerate(SLOTS)) for n in range(4))
    dy, dz, dc, dx = picks
    return ((zhi ^ dz) * 8 + ((y + dy) & 3) * 2 + (c ^ dc ^ (dx & odd))).astype(jnp.int32)


def shards(control, perturb, member_weights, blocks, block_cols, vertical):
    nodes_all, mem_dev, lev_dev = control.shape
    members_all = mem_dev * 16
    groups, owned = 8, nodes_all // 128
    core_index = lax.axis_index("core")
    core = core_index.reshape(1).astype(jnp.int32)
    other = 1 - core
    stored = blocks[:, 0]
    give, own = pack(core, stored)
    stages = gather(own, send(give, CORE))
    x = control.transpose(1, 2, 0).reshape(mem_dev * lev_dev, nodes_all)
    x_other = send(x, CORE)
    xc = prep_call(core, x, x_other)
    weights = member_weights / math.sqrt(members_all - 1)
    weights_other = send(weights, CORE)
    fields = perturb.transpose(0, 2, 1, 3)
    fields_other = send(fields, CORE)
    shape = (groups, 2, owned) + fields.shape[1:]
    fields, fields_other = fields.reshape(shape), fields_other.reshape(shape)
    table = slot_table()
    shape = (2, nodes_all // 2, nodes_all // 2)
    gx = lax.axis_index("x").reshape(1).astype(jnp.int32)
    gz = lax.axis_index("zlo").reshape(1).astype(jnp.int32)
    dense, halves = None, ()
    for stage, parts in enumerate(stages):
        pieces, plan = [p[0] for p in parts], tuple(p[1:] for p in parts)
        args = (block_cols.T, core, table, gx, gz, pieces, plan, shape)
        dense = place_call(*args, dense, halves)
        if stage >= len(stages) - 2:
            halves += (forward_call(xc, dense, len(halves) * shape[2] // 2),)
    parts = [REACH[a:b] for a, b in zip(CUTS, CUTS[1:])]
    ready, sums, last = [], [], ()
    for n in range(len(parts) + 1):
        if n < len(parts):
            give = backward_call(other, gx, gz, parts[n], *halves, dense, after=last)
            last = (give,)
            sums.append(send(give, CORE))
        if n > 0:
            keep = backward_call(core, gx, gz, parts[n - 1], *halves, dense, (sums[n - 1],), last)
            ready += keep
            last = (keep[0],)
    sources = []
    for value, pairs in zip(ready, LEVELS[:-1]):
        sources.append(send(value, pairs))
    sources.append(ready[-1])
    out = post_call(
        core, weights, weights_other, gx, gz, vertical, fields, fields_other, sources
    )
    out = lax.all_to_all(out, ("zhi", "y"), split_axis=0, concat_axis=0, tiled=True)
    return jnp.sum(out, axis=0).transpose(1, 0, 2)


def solution(mesh):
    fine = Mesh(mesh.devices.reshape(4, 2, 2, 4, 2), AXES)
    lev, mem = ("x", "zlo"), ("zhi", "y", "core")
    in_specs = (
        P(None, mem, lev),
        P(lev, mem, None, None),
        P(mem),
        P(None, mem, None, None),
        P(),
        P(),
    )
    out_specs = P(AXES, None, None)

    return jax.shard_map(shards, mesh=fine, in_specs=in_specs, out_specs=out_specs, check_vma=False)
```
